32 devices in a mesh: dp: 4 (over z), row: 2 (over x), col: 4 (over y, core).
Axes of the slice: x: 2, y: 2, z: 4, core: 2. Of those that a mesh axis runs over, the one named last changes fastest.
Arguments:
- layer_input: bfloat16 [16384, 2048], P(('dp', 'row'), 'col'), may hold values from -6 to 6
- norm1_gain: float32 [2048], P('col'), may hold values from 0.5 to 1.5
- norm1_shift: float32 [2048], P('col'), may hold values from -3 to 3
- w_query: bfloat16 [2048, 2048], P('col', 'row'), may hold values from -0.125 to 0.125
- b_query: float32 [2048], P('row'), may hold values from -3 to 3
- w_keyval: bfloat16 [2048, 256], P('col'), may hold values from -0.125 to 0.125
- b_value: float32 [128], replicated, may hold values from -3 to 3
- w_attn_out: bfloat16 [2048, 2048], P('row', 'col'), may hold values from -3 to 3
- b_attn_out: float32 [2048], P('col'), may hold values from -3 to 3
- norm2_gain: float32 [2048], P('col'), may hold values from 0.5 to 1.5
- norm2_shift: float32 [2048], P('col'), may hold values from -3 to 3
- w_fc_in: bfloat16 [2048, 8192], P('col', 'row'), may hold values from -0.125 to 0.125
- b_fc_in: float32 [8192], P('row'), may hold values from -3 to 3
- w_fc_out: bfloat16 [8192, 2048], P('row', 'col'), may hold values from -0.125 to 0.125
- b_fc_out: float32 [2048], P('col'), may hold values from -3 to 3
- valid_mask: int32 [4, 4096], P('dp'), may hold values from 0 to 1, as said below
- block_ids: int32 [4, 4096], P('dp'), may hold values from 0 to 31, never falling along the last dimension, each value on 1 to 256 neighbouring positions
- teacher: bfloat16 [16384, 2048], P(('dp', 'row'), 'col'), may hold values from -6 to 6
- out_cotangent: bfloat16 [16384, 2048], P(('dp', 'row'), 'col'), may hold values from -6 to 6
Outputs:
- layer_output: float32 [16384, 2048], P(('dp', 'row'), 'col')
- loss_value: float32 [], replicated
- input_grad: float32 [16384, 2048], P(('dp', 'row'), 'col')
- grad_norm1_gain: float32 [2048], P('col')
- grad_norm1_shift: float32 [2048], P('col')
- grad_w_query: float32 [2048, 2048], P('col', 'row')
- grad_b_query: float32 [2048], P('row')
- grad_w_keyval: float32 [2048, 256], P('col')
- grad_b_value: float32 [128], replicated
- grad_w_attn_out: float32 [2048, 2048], P('row', 'col')
- grad_b_attn_out: float32 [2048], P('col')
- grad_norm2_gain: float32 [2048], P('col')
- grad_norm2_shift: float32 [2048], P('col')
- grad_w_fc_in: float32 [2048, 8192], P('col', 'row')
- grad_b_fc_in: float32 [8192], P('row')
- grad_w_fc_out: float32 [8192, 2048], P('row', 'col')
- grad_b_fc_out: float32 [2048], P('col')
The draws below stay inside these ranges and needn't reach their ends.
Inputs may be any that keep to these rules, and one draw needn't show every extreme that they name: `valid_mask`: in each sequence the ones form a prefix of 1024 to 4096 positions and zeros follow; the first sequence has no padding. `block_ids`: within each sequence block numbers never fall along positions; each block holds 1 to 256 positions.
All inputs are finite; a program needn't handle non-finite values.
Results may differ from the reference program's by a relative error of at most 0.0034.
Values may be sent and summed in bfloat16 or wider, within the bound.
No kernel may reach another device: no remote copies, remote signals or barrier semaphores. Data moves between devices by JAX's collectives and lax.ppermute only.
A program may use at most 448 MiB of HBM per device.

```python
import math
import jax
import jax.numpy as jnp
import numpy as np
from jax import lax

D = 2048
HEADS = 16
HEAD = 128
FF = 8192
SEQ = 4096
BLOCK = 256
QROWS = 512
HQ = 2048
NBLK = 32
SEQS = 4
TOKENS = 16384


def draw_valid_mask(key, part):
    lengths = jax.random.randint(key, (SEQS,), SEQ // 4, SEQ + 1)
    lengths = lengths.at[0].set(SEQ)
    positions = jnp.arange(SEQ)
    return (positions[None, :] < lengths[:, None]).astype(jnp.int32)


def draw_out_cotangent(key, part):
    random_key = jax.random.fold_in(key, 11)
    shared_key = jax.random.fold_in(key, 12)
    shared_part = jax.random.normal(shared_key, (1, D), jnp.float32)
    random_part = jax.random.normal(random_key, (TOKENS, D), jnp.float32)
    values = random_part + 0.5 * shared_part
    return jnp.clip(values, -6.0, 6.0).astype(jnp.bfloat16)


def shard_levels(own_key, shape, cuts, low, largest):
    level, own = 1.0, jax.random.fold_in(own_key, 6)
    for axis_at, shards_of in cuts:
        steps = jnp.exp(jax.random.uniform(jax.random.fold_in(own, axis_at), (shards_of,), jnp.float32, low / len(cuts), largest / len(cuts)))
        level = level * jnp.repeat(steps, shape[axis_at] // shards_of).reshape([-1 if axis == axis_at else 1 for axis in range(len(shape))])
    return level


def length_profile(amount, total, most, lean):
    loads = [(1 << 20) // math.isqrt(rank ** lean) + 1 for rank in range(2, amount + 1)]
    rest, counts = total - most - (amount - 1), [1] * (amount - 1)
    while rest > 0:
        movable = [i for i in range(amount - 1) if counts[i] < most]
        pool, remaining = sum([loads[i] for i in movable]), rest
        for i in movable:
            more = min(most - counts[i], max(1, remaining * loads[i] // pool), rest)
            counts[i] = counts[i] + more
            rest = rest - more
    return np.array([most] + counts)


def uneven(stream_key, count, total, limit, slope):
    if count == 2:
        one = jax.random.randint(stream_key, (), max(1, total - limit), min(limit, total - 1) + 1)
        return jnp.stack([one, total - one])
    tallies = jnp.asarray(length_profile(count, total, limit, slope), jnp.int32)
    pairs = (count - 1) // 2
    donor, taker = tallies[1:1 + 2 * pairs:2], tallies[2:2 + 2 * pairs:2]
    slack = jnp.minimum(donor - 1, limit - taker)
    passed = jax.random.randint(jax.random.fold_in(stream_key, 1), (pairs,), 0, 1 << 20) % (slack + 1)
    tallies = tallies.at[1:1 + 2 * pairs:2].set(donor - passed).at[2:2 + 2 * pairs:2].set(taker + passed)
    return tallies[jax.random.permutation(jax.random.fold_in(stream_key, 2), count)]


def normal_values(stream_key, extent, spread, most, cuts=(), kind=jnp.bfloat16):
    values = jax.random.normal(stream_key, extent, jnp.float32) * spread
    if len(cuts) > 0:
        values = shard_levels(stream_key, extent, cuts, -0.22, 0.18) * values
    return jnp.clip(values, min=-most, max=most).astype(kind)


def setup_inputs(seed: int = 0) -> dict:
    key_of = jax.random.split(jax.random.key(seed), 20)
    layer_input = normal_values(key_of[0], (TOKENS, D), 1.0, 6.0, ((0, 8), (1, 4)))
    norm1_gain = jnp.clip(1.0 + 0.1 * jax.random.normal(key_of[1], (D,), jnp.float32), 0.5, 1.5)
    norm1_shift = normal_values(key_of[2], (D,), 0.3, 3.0, ((0, 4),), jnp.float32)
    w_query = normal_values(key_of[3], (D, HQ), D ** -0.5, 0.125, ((0, 4), (1, 2)))
    b_query = normal_values(key_of[4], (HQ,), 0.3, 3.0, ((0, 2),), jnp.float32)
    w_keyval = normal_values(key_of[5], (D, 2 * HEAD), D ** -0.5, 0.125, ((0, 4),))
    b_value = normal_values(key_of[6], (HEAD,), 0.3, 3.0, (), jnp.float32)
    w_attn_out = normal_values(key_of[7], (HQ, D), 4 ** -0.5, 3.0, ((0, 2), (1, 4)))
    b_attn_out = normal_values(key_of[8], (D,), 0.3, 3.0, ((0, 4),), jnp.float32)
    norm2_gain = jnp.clip(1.0 + 0.1 * jax.random.normal(key_of[9], (D,), jnp.float32), 0.5, 1.5)
    norm2_shift = normal_values(key_of[10], (D,), 0.3, 3.0, ((0, 4),), jnp.float32)
    w_fc_in = normal_values(key_of[11], (D, FF), D ** -0.5, 0.125, ((0, 4), (1, 2)))
    b_fc_in = normal_values(key_of[12], (FF,), 0.3, 3.0, ((0, 2),), jnp.float32)
    w_fc_out = normal_values(key_of[13], (FF, D), (FF // 4) ** -0.5, 0.125, ((0, 2), (1, 4)))
    b_fc_out = normal_values(key_of[14], (D,), 0.3, 3.0, ((0, 4),), jnp.float32)
    valid_mask = draw_valid_mask(jax.random.fold_in(key_of[19], 71), 0)
    block_ids = jax.vmap(lambda own: jnp.searchsorted(jnp.cumsum(uneven(own, NBLK, SEQ, BLOCK, 0)), jnp.arange(SEQ), side="right"))(jax.random.split(key_of[16], SEQS)).reshape((SEQS, SEQ)).astype(jnp.int32)
    teacher = normal_values(key_of[17], (TOKENS, D), 1.0, 6.0, ((0, 8), (1, 4)))
    out_cotangent = draw_out_cotangent(jax.random.fold_in(key_of[19], 71), 0)
    return dict(layer_input=layer_input, norm1_gain=norm1_gain, norm1_shift=norm1_shift, w_query=w_query, b_query=b_query, w_keyval=w_keyval, b_value=b_value, w_attn_out=w_attn_out, b_attn_out=b_attn_out, norm2_gain=norm2_gain, norm2_shift=norm2_shift, w_fc_in=w_fc_in, b_fc_in=b_fc_in, w_fc_out=w_fc_out, b_fc_out=b_fc_out, valid_mask=valid_mask, block_ids=block_ids, teacher=teacher, out_cotangent=out_cotangent)


@jax.custom_vjp
def low(v):
    return lax.optimization_barrier(v.astype(jnp.bfloat16)).astype(jnp.float32)

@jax.custom_vjp
def low_back(v):
    return v

def low_keep(v):
    return (low(v), None)

def low_pass(kept, grad):
    return (grad,)

def back_keep(v):
    return (v, None)

def back_low(kept, grad):
    return (low(grad),)
low.defvjp(low_keep, low_pass)
low_back.defvjp(back_keep, back_low)
epsilon = 1e-05
gelu_coeff = 0.7978845608028654

def gelu_tanh(values):
    return 0.5 * values * (1.0 + jnp.tanh(gelu_coeff * (values + 0.044715 * values * values * values)))

def matmul_high(left, right):
    return jnp.dot(left, right, precision=lax.Precision.HIGHEST, preferred_element_type=jnp.float32)

def layer_norm(values, gain, shift):
    means = lax.optimization_barrier(jnp.mean(values, 1, keepdims=True))
    variance = lax.optimization_barrier(jnp.mean(values * values, 1, keepdims=True)) - means * means
    return (values - means) * lax.rsqrt(variance + epsilon) * gain + shift

def reference(layer_input, norm1_gain, norm1_shift, w_query, b_query, w_keyval, b_value, w_attn_out, b_attn_out, norm2_gain, norm2_shift, w_fc_in, b_fc_in, w_fc_out, b_fc_out, valid_mask, block_ids, teacher, out_cotangent):
    valid_flat = valid_mask.reshape(-1)
    block_flat = block_ids.reshape(-1)
    valid_float = valid_flat.astype(jnp.float32)
    valid_count = jnp.sum(valid_float)
    target = teacher.astype(jnp.float32)
    score_scale = HEAD ** (-0.5)
    starts = (jnp.arange(TOKENS // QROWS) * QROWS).astype(jnp.int32)

    def attend_block(query_block, start, key_all, value_all):
        key_start = (start // SEQ * SEQ).astype(jnp.int32)
        key_block = lax.dynamic_slice_in_dim(key_all, key_start, SEQ, 0)
        value_block = lax.dynamic_slice_in_dim(value_all, key_start, SEQ, 0)
        query_ids = lax.dynamic_slice_in_dim(block_flat, start, QROWS, 0)
        key_ids = lax.dynamic_slice_in_dim(block_flat, key_start, SEQ, 0)
        key_valid = lax.dynamic_slice_in_dim(valid_flat, key_start, SEQ, 0)
        allowed = (key_ids[None, :] <= query_ids[:, None]) & (key_valid[None, :] > 0)
        raw_scores = low_back(jnp.einsum('qhd,kd->hqk', query_block, key_block, precision=lax.Precision.HIGHEST))
        scores = jnp.where(allowed[None], raw_scores * score_scale, -1e+30)
        maxima = lax.optimization_barrier(jnp.max(scores, -1, keepdims=True))
        exp_scores = jnp.where(allowed[None], jnp.exp(scores - maxima), 0.0)
        totals = lax.optimization_barrier(jnp.sum(exp_scores, -1, keepdims=True))
        probs = exp_scores / totals
        attended = jnp.einsum('hqk,kd->qhd', low(probs), value_block, precision=lax.Precision.HIGHEST)
        return attended.reshape(QROWS, HEADS * HEAD)
    block_step = jax.checkpoint(attend_block)

    def forward(inputs, gain_first, shift_first, wq_full, bq_full, wkv_full, bv_full, wo_full, bo_full, gain_second, shift_second, fc_in_full, fc_in_bias, fc_out_full, fc_out_bias):
        normed1 = low(layer_norm(inputs, gain_first, shift_first))
        queries = low(low_back(matmul_high(normed1, wq_full) + bq_full))
        keyval = matmul_high(normed1, wkv_full)
        key_all = low(low_back(keyval[:, :HEAD]))
        value_all = low(low_back(keyval[:, HEAD:] + bv_full))
        query_blocks = queries.reshape(TOKENS // QROWS, QROWS, HEADS, HEAD)
        attended = lax.map(lambda operands: block_step(operands[0], operands[1], key_all, value_all), (query_blocks, starts))
        attended = low(low_back(attended.reshape(TOKENS, HEADS * HEAD)))
        middle = inputs + low_back(matmul_high(attended, wo_full) + bo_full)
        normed2 = low(layer_norm(middle, gain_second, shift_second))
        activated = low(gelu_tanh(low_back(matmul_high(normed2, fc_in_full) + fc_in_bias)))
        output = middle + low_back(matmul_high(activated, fc_out_full) + fc_out_bias)
        errors = output - target
        loss_value = jnp.sum(valid_float[:, None] * errors * errors) / (valid_count * D)
        return (output, loss_value)
    primals = tuple((item.astype(jnp.float32) for item in (layer_input, norm1_gain, norm1_shift, w_query, b_query, w_keyval, b_value, w_attn_out, b_attn_out, norm2_gain, norm2_shift, w_fc_in, b_fc_in, w_fc_out, b_fc_out)))
    (layer_output, loss_value), pullback = jax.vjp(forward, *primals)
    loss_weight = jnp.asarray(TOKENS * D / 2.0, dtype=jnp.float32)
    grads = pullback((out_cotangent.astype(jnp.float32), loss_weight))
    return (layer_output, loss_value, grads[0], grads[1], grads[2], grads[3], grads[4], grads[5], grads[6], grads[7], grads[8], grads[9], grads[10], grads[11], grads[12], grads[13], grads[14])
```

```python
import functools
import jax, jax.numpy as jnp
from jax import lax
from jax.experimental import pallas as pl
from jax.experimental.pallas import tpu as pltpu
from jax.sharding import PartitionSpec as P

D = 2048
HEAD = 128
SCALE = HEAD**-0.5
SC = SCALE * 1.4426950408889634
NT = (((1,), (1,)), ((), ()))
NN = (((1,), (0,)), ((), ()))
TN = (((0,), (0,)), ((), ()))
f32 = jnp.float32
bf16 = jnp.bfloat16


def stack_heads(ref, heads):
    return jnp.concatenate([ref[:, h * HEAD : (h + 1) * HEAD] for h in range(heads)], axis=0)


def key_rows(ref, slot_ref, block, per_block, chunk):
    parts = [
        ref[pl.ds(pl.multiple_of(slot_ref[block * per_block + s] * chunk, chunk), chunk), :]
        for s in range(per_block)
    ]
    return parts[0] if per_block == 1 else jnp.concatenate(parts, axis=0)


def fwd_kernel(
    full_ref, count_ref, slot_ref, q_ref, k_ref, v_ref, lim_ref, o_ref, lse_ref, acc, top, tot,
    *, heads, tq, chunk, per_block
):
    t = pl.program_id(0)
    bk = chunk * per_block
    q = stack_heads(q_ref, heads)
    acc[...] = jnp.zeros_like(acc)
    top[...] = jnp.full_like(top, -1e30)
    tot[...] = jnp.zeros_like(tot)

    def step(block, masked):
        kk = key_rows(k_ref, slot_ref, block, per_block, chunk)
        vv = key_rows(v_ref, slot_ref, block, per_block, chunk)
        s = lax.dot_general(kk, q, NT, preferred_element_type=f32)
        if masked:
            ids = lax.broadcasted_iota(jnp.int32, (bk, heads * tq), 0) + block * bk
            lim = jnp.concatenate([lim_ref[:1, :]] * heads, axis=1)
            s = jnp.where(ids < lim, s, -1e30)
        before = top[...]
        now = jnp.maximum(before, jnp.max(s, axis=0, keepdims=True))
        p = jnp.exp2(s * SC - now * SC)
        top[...] = now
        a = jnp.exp2((before - now) * SC)
        tot[...] = tot[...] * a + jnp.sum(p, axis=0, keepdims=True)
        acc[...] = acc[...] * a + lax.dot_general(
            vv, p.astype(bf16), TN, preferred_element_type=f32
        )

    lax.fori_loop(0, full_ref[t], lambda b, c: (step(b, False), c)[1], 0)
    lax.fori_loop(full_ref[t], count_ref[t], lambda b, c: (step(b, True), c)[1], 0)
    o = acc[...] * (1.0 / tot[...])
    lse = top[...] * SC + jnp.log2(tot[...])
    for h in range(heads):
        o_ref[:, h * HEAD : (h + 1) * HEAD] = jnp.transpose(o[:, h * tq : (h + 1) * tq]).astype(bf16)
        lse_ref[h : h + 1, :] = lse[:, h * tq : (h + 1) * tq]


def bwd_kernel(
    full_ref, count_ref, slot_ref, q_ref, do_ref, k_ref, v_ref, lim_ref, lse_ref, dl_ref,
    dq_ref, dk_ref, dv_ref, dqa, *, heads, tq, chunk, per_block
):
    t = pl.program_id(0)
    bk = chunk * per_block

    @pl.when((t == 0) & (pl.program_id(1) == 0))
    def _():
        dk_ref[...] = jnp.zeros_like(dk_ref)
        dv_ref[...] = jnp.zeros_like(dv_ref)

    q = stack_heads(q_ref, heads)
    do = stack_heads(do_ref, heads)
    lse = jnp.concatenate([lse_ref[h : h + 1, :] for h in range(heads)], axis=1)
    dl = jnp.concatenate([dl_ref[h : h + 1, :] for h in range(heads)], axis=1)
    dqa[...] = jnp.zeros_like(dqa)

    def step(block, masked):
        kk = key_rows(k_ref, slot_ref, block, per_block, chunk)
        vv = key_rows(v_ref, slot_ref, block, per_block, chunk)
        s = lax.dot_general(kk, q, NT, preferred_element_type=f32)
        p = jnp.exp2(s * SC - lse)
        if masked:
            ids = lax.broadcasted_iota(jnp.int32, (bk, heads * tq), 0) + block * bk
            lim = jnp.concatenate([lim_ref[:1, :]] * heads, axis=1)
            p = jnp.where(ids < lim, p, 0.0)
        dp = lax.dot_general(vv, do, NT, preferred_element_type=f32)
        ds = (p * (dp - dl)).astype(bf16)
        dv = lax.dot_general(p.astype(bf16), do, NN, preferred_element_type=f32)
        dk = lax.dot_general(ds, q, NN, preferred_element_type=f32)
        dqa[...] += lax.dot_general(ds, kk, TN, preferred_element_type=f32)
        for s in range(per_block):
            off = pl.multiple_of(slot_ref[block * per_block + s] * chunk, chunk)
            dk_ref[pl.ds(off, chunk), :] += dk[s * chunk : (s + 1) * chunk]
            dv_ref[pl.ds(off, chunk), :] += dv[s * chunk : (s + 1) * chunk]

    lax.fori_loop(0, full_ref[t], lambda b, c: (step(b, False), c)[1], 0)
    lax.fori_loop(full_ref[t], count_ref[t], lambda b, c: (step(b, True), c)[1], 0)
    dq = (dqa[...] * HEAD**-0.5).astype(bf16)
    for h in range(heads):
        dq_ref[:, h * HEAD : (h + 1) * HEAD] = dq[h * tq : (h + 1) * tq]

    @pl.when((t == pl.num_programs(0) - 1) & (pl.program_id(1) == pl.num_programs(1) - 1))
    def _():
        dk_ref[...] = dk_ref[...] * HEAD**-0.5


def block_counts(limits, tq, bk):
    tiles = limits.reshape(-1, tq)
    return jnp.min(tiles, 1) // bk, (jnp.max(tiles, 1) + bk - 1) // bk


def attend_forward(q, k, v, limits, slots, chunk, tq=128, heads=16, bk=256):
    n, hq = q.shape
    total = hq // HEAD
    per_block = max(1, bk // chunk)
    full, count = block_counts(limits, tq, chunk * per_block)
    rows = k.shape[0]
    grid = pltpu.PrefetchScalarGridSpec(
        num_scalar_prefetch=3,
        grid=(n // tq, total // heads),
        in_specs=[
            pl.BlockSpec((tq, heads * HEAD), lambda t, g, *_: (t, g)),
            pl.BlockSpec((rows, HEAD), lambda t, g, *_: (0, 0)),
            pl.BlockSpec((rows, HEAD), lambda t, g, *_: (0, 0)),
            pl.BlockSpec((8, tq), lambda t, g, *_: (0, t)),
        ],
        out_specs=[
            pl.BlockSpec((tq, heads * HEAD), lambda t, g, *_: (t, g)),
            pl.BlockSpec((heads, tq), lambda t, g, *_: (g, t)),
        ],
        scratch_shapes=[
            pltpu.VMEM((HEAD, heads * tq), f32),
            pltpu.VMEM((1, heads * tq), f32),
            pltpu.VMEM((1, heads * tq), f32),
        ],
    )
    return pl.pallas_call(
        functools.partial(fwd_kernel, heads=heads, tq=tq, chunk=chunk, per_block=per_block),
        grid_spec=grid,
        out_shape=(jax.ShapeDtypeStruct((n, hq), bf16), jax.ShapeDtypeStruct((total, n), f32)),
        name="attend_forward",
        compiler_params=pltpu.CompilerParams(vmem_limit_bytes=48 << 20),
    )(full, count, slots, q, k, v, jnp.broadcast_to(limits[None, :], (8, n)))


def attend_backward(q, do, k, v, limits, slots, lse, delta, chunk, tq=128, heads=16, bk=256):
    n, hq = q.shape
    total = hq // HEAD
    per_block = max(1, bk // chunk)
    full, count = block_counts(limits, tq, chunk * per_block)
    rows = k.shape[0]
    token_block = pl.BlockSpec((tq, heads * HEAD), lambda t, g, *_: (t, g))
    key_block = pl.BlockSpec((rows, HEAD), lambda t, g, *_: (0, 0))
    head_block = pl.BlockSpec((heads, tq), lambda t, g, *_: (g, t))
    grid = pltpu.PrefetchScalarGridSpec(
        num_scalar_prefetch=3,
        grid=(n // tq, total // heads),
        in_specs=[
            token_block, token_block, key_block, key_block,
            pl.BlockSpec((8, tq), lambda t, g, *_: (0, t)),
            head_block, head_block,
        ],
        out_specs=[token_block, key_block, key_block],
        scratch_shapes=[pltpu.VMEM((heads * tq, HEAD), f32)],
    )
    return pl.pallas_call(
        functools.partial(bwd_kernel, heads=heads, tq=tq, chunk=chunk, per_block=per_block),
        grid_spec=grid,
        out_shape=(
            jax.ShapeDtypeStruct((n, hq), bf16),
            jax.ShapeDtypeStruct((rows, HEAD), f32),
            jax.ShapeDtypeStruct((rows, HEAD), f32),
        ),
        name="attend_backward",
        compiler_params=pltpu.CompilerParams(vmem_limit_bytes=48 << 20),
    )(full, count, slots, q, do, k, v, jnp.broadcast_to(limits[None, :], (8, n)), lse, delta)


epsilon = 1e-05
gelu_coeff = 0.7978845608028654


def send(x, axis, mask):
    size = lax.axis_size(axis)
    return lax.ppermute(x, axis, [(i, i ^ mask) for i in range(size)])


def send_pair(x, i, j):
    count_row, count_col = lax.axis_size("row"), lax.axis_size("col")
    pairs = [
        (a * count_col + b, (a ^ i) * count_col + (b ^ j))
        for a in range(count_row)
        for b in range(count_col)
    ]
    return lax.ppermute(x, ("row", "col"), pairs)


def masks_of(axis):
    size = lax.axis_size(axis)
    return [1 << k for k in reversed(range(size.bit_length() - 1))]


def other_key(key, axis, mask):
    return (key[0] ^ mask, key[1]) if axis == "row" else (key[0], key[1] ^ mask)


def gather_pieces(x, steps):
    pieces = {(0, 0): x}
    for axis, mask in steps:
        for key in list(pieces):
            pieces[other_key(key, axis, mask)] = send(pieces[key], axis, mask)
    return pieces


def reduce_pieces(pieces, steps, wire):
    pieces = dict(pieces)
    for axis, mask in steps:
        at = 0 if axis == "row" else 1
        for key in [key for key in pieces if key[at] & mask]:
            arrived = send(pieces.pop(key).astype(wire), axis, mask)
            home = other_key(key, axis, mask)
            pieces[home] = pieces[home].astype(f32) + arrived.astype(f32)
    return pieces[(0, 0)]


def join(pieces, rows, cols):
    strips = [
        jnp.concatenate([pieces[(i, j)] for i in range(rows)], 1) if rows > 1 else pieces[(0, j)]
        for j in range(cols)
    ]
    return jnp.concatenate(strips, 0) if cols > 1 else strips[0]


def everywhere(x, axes):
    for axis in axes:
        for mask in masks_of(axis):
            x = x + send(x, axis, mask)
    return x


def gelu_tanh(values):
    return (
        0.5 * values * (1.0 + jnp.tanh(gelu_coeff * (values + 0.044715 * values * values * values)))
    )


def gelu_slope(values):
    square = values * values
    curve = jnp.tanh(gelu_coeff * values * (1.0 + 0.044715 * square))
    return 0.5 * (1.0 + curve) + 0.5 * values * (1.0 - curve * curve) * gelu_coeff * (
        1.0 + 3.0 * 0.044715 * square
    )


def norm_forward(values, gain, shift):
    means = jnp.mean(values, 1, keepdims=True)
    squares = jnp.mean(values * values, 1, keepdims=True)
    inverse = lax.rsqrt(squares - means * means + epsilon)
    normal = (values - means) * inverse
    return (normal, inverse, (normal * gain + shift).astype(bf16))


def norm_backward(grad, normal, inverse, gain):
    scaled = grad * gain
    return inverse * (
        scaled
        - jnp.mean(scaled, 1, keepdims=True)
        - normal * jnp.mean(scaled * normal, 1, keepdims=True)
    )


def dot_nn(a, b):
    return lax.dot_general(a, b, NN, preferred_element_type=f32)


def dot_nt(a, b):
    return lax.dot_general(a, b, NT, preferred_element_type=f32)


def dot_tn(a, b):
    return lax.dot_general(a, b, TN, preferred_element_type=f32)


def chunk_rows(chunk, i, j):
    count_row, count_col = lax.axis_size("row"), lax.axis_size("col")
    r, c = lax.axis_index("row"), lax.axis_index("col") ^ j
    if count_row == 2:
        owner = (r ^ i) * count_col + c
        return jnp.where(r == 0, owner, 2 * count_col - 1 - owner) * chunk
    return (c if i == 0 else 2 * count_col - 1 - c) * chunk


def chunk_send(x, i, j):
    if lax.axis_size("row") == 2:
        return send_pair(x, i, j) if i or j else x
    return send(x, "col", j) if j else x


def to_tokens(block, chunk):
    count_col = lax.axis_size("col")
    return [
        [
            chunk_send(lax.dynamic_slice_in_dim(block, chunk_rows(chunk, i, j), chunk, 0), i, j)
            for j in range(count_col)
        ]
        for i in range(2)
    ]


def assemble(pieces):
    return jnp.concatenate([jnp.concatenate(strip, 1) for strip in pieces], 0)


def from_tokens(tokens, chunk, width, rows):
    out = jnp.zeros((rows, width), f32)
    low = tokens.astype(bf16)
    for i in range(2):
        for j in range(lax.axis_size("col")):
            part = low[i * chunk : (i + 1) * chunk, j * width : (j + 1) * width]
            out = lax.dynamic_update_slice_in_dim(
                out, chunk_send(part, i, j).astype(f32), chunk_rows(chunk, i, j), 0
            )
    return out


def token_starts(chunk):
    count_row, count_col = lax.axis_size("row"), lax.axis_size("col")
    r, c = lax.axis_index("row"), lax.axis_index("col")
    if count_row == 2:
        own = r * count_col + c
        low, high = own * chunk, (4 * count_col - 1 - own) * chunk
        return [jnp.where(r == 0, low, high), jnp.where(r == 0, high, low)]
    return [(r * 2 * count_col + c) * chunk, (r * 2 * count_col + 2 * count_col - 1 - c) * chunk]


def key_slots():
    count_row, count_col = lax.axis_size("row"), lax.axis_size("col")
    r, c = lax.axis_index("row"), lax.axis_index("col")
    group = jnp.arange(2 * count_row * count_col, dtype=jnp.int32)
    half = group // (2 * count_col)
    if count_row == 2:
        owner = jnp.where(half == 0, group, 4 * count_col - 1 - group)
        owner_row, owner_col = owner // count_col, owner % count_col
        which = owner_row ^ half
    else:
        local = group % (2 * count_col)
        owner_row = half
        which = (local >= count_col).astype(jnp.int32)
        owner_col = jnp.where(which == 0, local, 2 * count_col - 1 - local)
    return ((owner_row ^ r) * count_col + (owner_col ^ c)) * 2 + which


def over_dp(total, wire):
    size = lax.axis_size("dp")
    if size != 4:
        return everywhere(total, ["dp"])
    z = lax.axis_index("dp")
    half = total.shape[0] // 2
    total = total + lax.ppermute(total.astype(wire), "dp", [(0, 1), (3, 2)]).astype(f32)
    own_at = jnp.where(z < 2, 0, half)
    far_at = half - own_at
    middle = [(1, 2), (2, 1)]
    outward = [(1, 0), (2, 3)]
    far = lax.dynamic_slice_in_dim(total, far_at, half, 0).astype(wire)
    own = lax.dynamic_slice_in_dim(total, own_at, half, 0)
    own = (own + lax.ppermute(far, "dp", middle).astype(f32)).astype(wire)
    far = lax.ppermute(own, "dp", middle)
    own_out = lax.ppermute(own, "dp", outward)
    far_out = lax.ppermute(far, "dp", outward)
    inside = (z == 1) | (z == 2)
    own = jnp.where(inside, own, own_out).astype(f32)
    far = jnp.where(inside, far, far_out).astype(f32)
    first = jnp.where(z < 2, own, far)
    second = jnp.where(z < 2, far, own)
    return jnp.concatenate([first, second], 0)


def per_device(
    layer_input,
    norm1_gain,
    norm1_shift,
    w_query,
    b_query,
    w_keyval,
    b_value,
    w_attn_out,
    b_attn_out,
    norm2_gain,
    norm2_shift,
    w_fc_in,
    b_fc_in,
    w_fc_out,
    b_fc_out,
    valid_mask,
    block_ids,
    teacher,
    out_cotangent,
):
    count_row = lax.axis_size("row")
    count_col = lax.axis_size("col")
    count_dp = lax.axis_size("dp")
    rows_a, width = layer_input.shape
    wide = w_query.shape[1]
    chunk = rows_a // (2 * count_col)
    col_in = [("col", m) for m in masks_of("col")]
    row_in = [("row", m) for m in masks_of("row")]
    col_out, row_out = col_in[::-1], row_in[::-1]
    near, across = col_in[-1:], col_in[:-1]
    all_in = across + row_in + near
    all_out = near + row_out + across[::-1]
    valid_flat = valid_mask.reshape(-1)
    block_flat = block_ids.reshape(-1)

    x_pieces = to_tokens(layer_input, chunk)
    vectors = gather_pieces(
        jnp.stack([norm1_gain, norm1_shift, b_attn_out, norm2_gain, norm2_shift, b_fc_out]), col_in
    )
    vectors = jnp.concatenate([vectors[(0, j)] for j in range(count_col)], 1)
    gain1, shift1, bias_o, gain2, shift2, bias_out = [vectors[k : k + 1] for k in range(6)]
    bias_q = gather_pieces(b_query[None, :], row_in)
    bias_q = jnp.concatenate([bias_q[(i, 0)] for i in range(count_row)], 1)
    keyval_w = join(gather_pieces(w_keyval, col_in), 1, count_col)
    query_w = join(gather_pieces(w_query, all_in), count_row, count_col)
    attn_pieces = gather_pieces(w_attn_out, all_in)
    attn_w = jnp.concatenate(
        [
            jnp.concatenate([attn_pieces[(i, j)] for j in range(count_col)], 1)
            for i in range(count_row)
        ],
        0,
    )
    fc_in_pieces = gather_pieces(w_fc_in, col_in)
    fc_in_w = jnp.concatenate([fc_in_pieces[(0, j)] for j in range(count_col)], 0)
    fc_out_pieces = gather_pieces(w_fc_out, col_in)
    fc_out_w = jnp.concatenate([fc_out_pieces[(0, j)] for j in range(count_col)], 1)
    late_pieces = [
        [
            chunk_send(
                jnp.concatenate(
                    [
                        lax.dynamic_slice_in_dim(block, chunk_rows(chunk, i, j), chunk, 0)
                        for block in (teacher, out_cotangent)
                    ],
                    0,
                ),
                i,
                j,
            )
            for j in range(count_col)
        ]
        for i in range(2)
    ]
    target = assemble([[piece[:chunk] for piece in strip] for strip in late_pieces])
    cotangent = assemble([[piece[chunk:] for piece in strip] for strip in late_pieces])

    starts = token_starts(chunk)
    block_own = jnp.concatenate(
        [lax.dynamic_slice_in_dim(block_flat, start, chunk, 0) for start in starts]
    )
    valid_own = jnp.concatenate(
        [lax.dynamic_slice_in_dim(valid_flat, start, chunk, 0) for start in starts]
    ).astype(f32)[:, None]
    valid_length = jnp.sum(valid_flat)
    reach = jnp.sum((block_flat[None, :] <= block_own[:, None]).astype(jnp.int32), 1)
    limits = jnp.minimum(reach, valid_length)
    slots = key_slots()
    valid_count = everywhere(jnp.full((8, 128), valid_length.astype(f32)), ["dp"])[0, 0]

    residual = assemble(x_pieces).astype(f32)
    normal1, inverse1, normed1 = norm_forward(residual, gain1, shift1)
    keyval = dot_nn(normed1, keyval_w)
    keyval = jnp.concatenate(
        [keyval[:, :HEAD].astype(bf16), (keyval[:, HEAD:] + b_value).astype(bf16)], 1
    )
    keyval_pieces = gather_pieces(keyval, all_in)
    keyval_all = jnp.concatenate(
        [keyval_pieces[(i, j)] for i in range(count_row) for j in range(count_col)], 0
    )
    keys, values = keyval_all[:, :HEAD], keyval_all[:, HEAD:]
    queries = (dot_nn(normed1, query_w) + bias_q).astype(bf16)
    attended, log_totals = attend_forward(queries, keys, values, limits, slots, chunk)
    middle = residual + (dot_nn(attended, attn_w) + bias_o)
    normal2, inverse2, normed2 = norm_forward(middle, gain2, shift2)
    own = normed2.shape[0]

    def row_gather(x):
        pieces = gather_pieces(x, row_in)
        return jnp.concatenate([pieces[(i, 0)] for i in range(count_row)], 0)

    def row_sum(x):
        pieces = {(i, 0): x[i * own : (i + 1) * own] for i in range(count_row)}
        return reduce_pieces(pieces, row_out, bf16)

    normed2_all = row_gather(normed2)
    pre_act = dot_nn(normed2_all, fc_in_w) + b_fc_in
    act = gelu_tanh(pre_act).astype(bf16)
    layer_output = middle + (row_sum(dot_nn(act, fc_out_w)) + bias_out)
    errors = layer_output - target.astype(f32)
    loss_part = jnp.sum(valid_own * errors * errors)
    ratio = rows_a * count_row * count_dp / valid_count
    grad_out = cotangent.astype(f32) + ratio * valid_own * errors
    output_block = from_tokens(layer_output, chunk, width, rows_a)
    grad_mlp = grad_out.astype(bf16)
    grad_fc_out_bias = jnp.sum(grad_mlp, 0, dtype=f32)
    grad_mlp_all = row_gather(grad_mlp)

    parts = 2
    hidden = act.shape[1] // parts
    fc_out_grads = []
    for f in range(parts):
        pieces = {
            (0, j): dot_tn(
                act[:, f * hidden : (f + 1) * hidden],
                grad_mlp_all[:, j * width : (j + 1) * width],
            )
            for j in range(count_col)
        }
        fc_out_grads.append(over_dp(reduce_pieces(pieces, col_out, bf16), bf16))
    grad_fc_out = jnp.concatenate(fc_out_grads, 0)

    grad_pre = (dot_nt(grad_mlp_all, fc_out_w) * gelu_slope(pre_act)).astype(bf16)
    grad_fc_in_bias = jnp.sum(grad_pre, 0, dtype=f32)
    grad_normed2 = row_sum(dot_nt(grad_pre, fc_in_w))
    fc_in_grads = []
    for f in range(parts):
        pieces = {
            (0, j): dot_tn(
                normed2_all[:, j * width : (j + 1) * width],
                grad_pre[:, f * hidden : (f + 1) * hidden],
            )
            for j in range(count_col)
        }
        fc_in_grads.append(over_dp(reduce_pieces(pieces, col_out, bf16), bf16))
    grad_fc_in = jnp.concatenate(fc_in_grads, 1)

    gain2_part = jnp.sum(grad_normed2 * normal2, 0)
    shift2_part = jnp.sum(grad_normed2, 0)
    grad_middle = grad_out + norm_backward(grad_normed2, normal2, inverse2, gain2)
    grad_attn = grad_middle.astype(bf16)
    grad_attn_bias = jnp.sum(grad_attn, 0, dtype=f32)
    pieces = {
        (i, j): dot_tn(
            attended[:, i * wide : (i + 1) * wide], grad_attn[:, j * width : (j + 1) * width]
        )
        for i in range(count_row)
        for j in range(count_col)
    }
    grad_attn_out = over_dp(reduce_pieces(pieces, all_out, bf16), bf16)
    grad_attended = dot_nt(grad_attn, attn_w).astype(bf16)

    heads = queries.shape[1] // HEAD
    delta = jnp.sum(
        (attended.astype(f32) * grad_attended.astype(f32)).reshape(own, heads, HEAD), -1
    ).T
    grad_queries, grad_keys, grad_values = attend_backward(
        queries, grad_attended, keys, values, limits, slots, log_totals, delta, chunk
    )
    grad_keyval = jnp.concatenate([grad_keys, grad_values], 1)
    pieces = {
        (i, j): grad_keyval[(i * count_col + j) * own : (i * count_col + j + 1) * own]
        for i in range(count_row)
        for j in range(count_col)
    }
    grad_keyval_low = reduce_pieces(pieces, all_out, f32).astype(bf16)
    grad_value_bias = jnp.sum(grad_keyval_low[:, HEAD:], 0, dtype=f32)
    grad_query_bias = jnp.sum(grad_queries, 0, dtype=f32)
    pieces = {
        (i, j): dot_tn(
            normed1[:, j * width : (j + 1) * width], grad_queries[:, i * wide : (i + 1) * wide]
        )
        for i in range(count_row)
        for j in range(count_col)
    }
    grad_query_w = over_dp(reduce_pieces(pieces, all_out, bf16), bf16)
    pieces = {
        (0, j): dot_tn(normed1[:, j * width : (j + 1) * width], grad_keyval_low)
        for j in range(count_col)
    }
    grad_keyval_w = everywhere(reduce_pieces(pieces, col_out, f32), ["row", "dp"])
    grad_normed1 = dot_nt(grad_queries, query_w) + dot_nt(grad_keyval_low, keyval_w)
    gain1_part = jnp.sum(grad_normed1 * normal1, 0)
    shift1_part = jnp.sum(grad_normed1, 0)
    input_grad = grad_middle + norm_backward(grad_normed1, normal1, inverse1, gain1)
    input_block = from_tokens(input_grad, chunk, width, rows_a)

    def feature_sums(parts_list):
        stacked = jnp.stack(parts_list)
        pieces = {(0, j): stacked[:, j * width : (j + 1) * width] for j in range(count_col)}
        return everywhere(reduce_pieces(pieces, col_out, f32), ["row", "dp"])

    early = feature_sums([gain2_part, shift2_part, grad_fc_out_bias, grad_attn_bias])
    late = feature_sums([gain1_part, shift1_part])
    loss_sum = everywhere(jnp.full((8, 128), loss_part), ["row", "col", "dp"])[0, 0]
    fc_in_bias_sum = everywhere(grad_fc_in_bias[None, :], ["col", "dp"])[0]
    pieces = {(i, 0): grad_query_bias[None, i * wide : (i + 1) * wide] for i in range(count_row)}
    query_bias_sum = everywhere(reduce_pieces(pieces, row_out, f32), ["col", "dp"])[0]
    value_bias_sum = everywhere(grad_value_bias[None, :], ["row", "col", "dp"])[0]
    return (
        output_block,
        loss_sum / (valid_count * D),
        input_block,
        late[0],
        late[1],
        grad_query_w,
        query_bias_sum,
        grad_keyval_w,
        value_bias_sum,
        grad_attn_out,
        early[3],
        early[0],
        early[1],
        grad_fc_in,
        fc_in_bias_sum,
        grad_fc_out,
        early[2],
    )


def solution(mesh):
    placed = (
        P(("dp", "row"), "col"),
        P("col"),
        P("col"),
        P("col", "row"),
        P("row"),
        P("col", None),
        P(),
        P("row", "col"),
        P("col"),
        P("col"),
        P("col"),
        P("col", "row"),
        P("row"),
        P("row", "col"),
        P("col"),
        P("dp", None),
        P("dp", None),
        P(("dp", "row"), "col"),
        P(("dp", "row"), "col"),
    )
    return jax.shard_map(
        per_device,
        mesh=mesh,
        in_specs=placed,
        out_specs=(
            P(("dp", "row"), "col"),
            P(),
            P(("dp", "row"), "col"),
            P("col"),
            P("col"),
            P("col", "row"),
            P("row"),
            P("col", None),
            P(),
            P("row", "col"),
            P("col"),
            P("col"),
            P("col"),
            P("col", "row"),
            P("row"),
            P("row", "col"),
            P("col"),
        ),
        check_vma=False,
    )
```

```python
import functools
import jax, jax.numpy as jnp
from jax import lax
from jax.experimental import pallas as pl
from jax.experimental.pallas import tpu as pltpu
from jax.sharding import PartitionSpec as P

D = 2048
HEAD = 128
SCALE = HEAD**-0.5
SC = SCALE * 1.4426950408889634
NT = (((1,), (1,)), ((), ()))
NN = (((1,), (0,)), ((), ()))
TN = (((0,), (0,)), ((), ()))
f32 = jnp.float32
bf16 = jnp.bfloat16


def stack_heads(ref, heads):
    return jnp.concatenate([ref[:, h * HEAD : (h + 1) * HEAD] for h in range(heads)], axis=0)


def key_rows(ref, slot_ref, block, per_block, chunk):
    parts = [
        ref[pl.ds(pl.multiple_of(slot_ref[block * per_block + s] * chunk, chunk), chunk), :]
        for s in range(per_block)
    ]
    return parts[0] if per_block == 1 else jnp.concatenate(parts, axis=0)


def fwd_kernel(
    full_ref, count_ref, slot_ref, q_ref, k_ref, v_ref, lim_ref, o_ref, lse_ref, acc, top, tot,
    *, heads, tq, chunk, per_block
):
    t = pl.program_id(0)
    bk = chunk * per_block
    q = stack_heads(q_ref, heads)
    acc[...] = jnp.zeros_like(acc)
    top[...] = jnp.full_like(top, -1e30)
    tot[...] = jnp.zeros_like(tot)

    def step(block, masked):
        kk = key_rows(k_ref, slot_ref, block, per_block, chunk)
        vv = key_rows(v_ref, slot_ref, block, per_block, chunk)
        s = lax.dot_general(kk, q, NT, preferred_element_type=f32)
        if masked:
            ids = lax.broadcasted_iota(jnp.int32, (bk, heads * tq), 0) + block * bk
            lim = jnp.concatenate([lim_ref[:1, :]] * heads, axis=1)
            s = jnp.where(ids < lim, s, -1e30)
        before = top[...]
        now = jnp.maximum(before, jnp.max(s, axis=0, keepdims=True))
        p = jnp.exp2(s * SC - now * SC)
        top[...] = now
        a = jnp.exp2((before - now) * SC)
        tot[...] = tot[...] * a + jnp.sum(p, axis=0, keepdims=True)
        acc[...] = acc[...] * a + lax.dot_general(
            vv, p.astype(bf16), TN, preferred_element_type=f32
        )

    lax.fori_loop(0, full_ref[t], lambda b, c: (step(b, False), c)[1], 0)
    lax.fori_loop(full_ref[t], count_ref[t], lambda b, c: (step(b, True), c)[1], 0)
    o = acc[...] * (1.0 / tot[...])
    lse = top[...] * SC + jnp.log2(tot[...])
    for h in range(heads):
        o_ref[:, h * HEAD : (h + 1) * HEAD] = jnp.transpose(o[:, h * tq : (h + 1) * tq]).astype(bf16)
        lse_ref[h : h + 1, :] = lse[:, h * tq : (h + 1) * tq]


def bwd_kernel(
    full_ref, count_ref, slot_ref, q_ref, do_ref, k_ref, v_ref, lim_ref, lse_ref, dl_ref,
    dq_ref, dk_ref, dv_ref, dqa, *, heads, tq, chunk, per_block
):
    t = pl.program_id(0)
    bk = chunk * per_block

    @pl.when((t == 0) & (pl.program_id(1) == 0))
    def _():
        dk_ref[...] = jnp.zeros_like(dk_ref)
        dv_ref[...] = jnp.zeros_like(dv_ref)

    q = stack_heads(q_ref, heads)
    do = stack_heads(do_ref, heads)
    lse = jnp.concatenate([lse_ref[h : h + 1, :] for h in range(heads)], axis=1)
    dl = jnp.concatenate([dl_ref[h : h + 1, :] for h in range(heads)], axis=1)
    dqa[...] = jnp.zeros_like(dqa)

    def step(block, masked):
        kk = key_rows(k_ref, slot_ref, block, per_block, chunk)
        vv = key_rows(v_ref, slot_ref, block, per_block, chunk)
        s = lax.dot_general(kk, q, NT, preferred_element_type=f32)
        p = jnp.exp2(s * SC - lse)
        if masked:
            ids = lax.broadcasted_iota(jnp.int32, (bk, heads * tq), 0) + block * bk
            lim = jnp.concatenate([lim_ref[:1, :]] * heads, axis=1)
            p = jnp.where(ids < lim, p, 0.0)
        dp = lax.dot_general(vv, do, NT, preferred_element_type=f32)
        ds = (p * (dp - dl)).astype(bf16)
        dv = lax.dot_general(p.astype(bf16), do, NN, preferred_element_type=f32)
        dk = lax.dot_general(ds, q, NN, preferred_element_type=f32)
        dqa[...] += lax.dot_general(ds, kk, TN, preferred_element_type=f32)
        for s in range(per_block):
            off = pl.multiple_of(slot_ref[block * per_block + s] * chunk, chunk)
            dk_ref[pl.ds(off, chunk), :] += dk[s * chunk : (s + 1) * chunk]
            dv_ref[pl.ds(off, chunk), :] += dv[s * chunk : (s + 1) * chunk]

    lax.fori_loop(0, full_ref[t], lambda b, c: (step(b, False), c)[1], 0)
    lax.fori_loop(full_ref[t], count_ref[t], lambda b, c: (step(b, True), c)[1], 0)
    dq = (dqa[...] * HEAD**-0.5).astype(bf16)
    for h in range(heads):
        dq_ref[:, h * HEAD : (h + 1) * HEAD] = dq[h * tq : (h + 1) * tq]

    @pl.when((t == pl.num_programs(0) - 1) & (pl.program_id(1) == pl.num_programs(1) - 1))
    def _():
        dk_ref[...] = dk_ref[...] * HEAD**-0.5


def block_counts(limits, tq, bk):
    tiles = limits.reshape(-1, tq)
    return jnp.min(tiles, 1) // bk, (jnp.max(tiles, 1) + bk - 1) // bk


def attend_forward(q, k, v, limits, slots, chunk, tq=128, heads=16, bk=256):
    n, hq = q.shape
    total = hq // HEAD
    per_block = max(1, bk // chunk)
    full, count = block_counts(limits, tq, chunk * per_block)
    rows = k.shape[0]
    grid = pltpu.PrefetchScalarGridSpec(
        num_scalar_prefetch=3,
        grid=(n // tq, total // heads),
        in_specs=[
            pl.BlockSpec((tq, heads * HEAD), lambda t, g, *_: (t, g)),
            pl.BlockSpec((rows, HEAD), lambda t, g, *_: (0, 0)),
            pl.BlockSpec((rows, HEAD), lambda t, g, *_: (0, 0)),
            pl.BlockSpec((8, tq), lambda t, g, *_: (0, t)),
        ],
        out_specs=[
            pl.BlockSpec((tq, heads * HEAD), lambda t, g, *_: (t, g)),
            pl.BlockSpec((heads, tq), lambda t, g, *_: (g, t)),
        ],
        scratch_shapes=[
            pltpu.VMEM((HEAD, heads * tq), f32),
            pltpu.VMEM((1, heads * tq), f32),
            pltpu.VMEM((1, heads * tq), f32),
        ],
    )
    return pl.pallas_call(
        functools.partial(fwd_kernel, heads=heads, tq=tq, chunk=chunk, per_block=per_block),
        grid_spec=grid,
        out_shape=(jax.ShapeDtypeStruct((n, hq), bf16), jax.ShapeDtypeStruct((total, n), f32)),
        name="attend_forward",
        compiler_params=pltpu.CompilerParams(vmem_limit_bytes=48 << 20),
    )(full, count, slots, q, k, v, jnp.broadcast_to(limits[None, :], (8, n)))


def attend_backward(q, do, k, v, limits, slots, lse, delta, chunk, tq=128, heads=16, bk=256):
    n, hq = q.shape
    total = hq // HEAD
    per_block = max(1, bk // chunk)
    full, count = block_counts(limits, tq, chunk * per_block)
    rows = k.shape[0]
    token_block = pl.BlockSpec((tq, heads * HEAD), lambda t, g, *_: (t, g))
    key_block = pl.BlockSpec((rows, HEAD), lambda t, g, *_: (0, 0))
    head_block = pl.BlockSpec((heads, tq), lambda t, g, *_: (g, t))
    grid = pltpu.PrefetchScalarGridSpec(
        num_scalar_prefetch=3,
        grid=(n // tq, total // heads),
        in_specs=[
            token_block, token_block, key_block, key_block,
            pl.BlockSpec((8, tq), lambda t, g, *_: (0, t)),
            head_block, head_block,
        ],
        out_specs=[token_block, key_block, key_block],
        scratch_shapes=[pltpu.VMEM((heads * tq, HEAD), f32)],
    )
    return pl.pallas_call(
        functools.partial(bwd_kernel, heads=heads, tq=tq, chunk=chunk, per_block=per_block),
        grid_spec=grid,
        out_shape=(
            jax.ShapeDtypeStruct((n, hq), bf16),
            jax.ShapeDtypeStruct((rows, HEAD), f32),
            jax.ShapeDtypeStruct((rows, HEAD), f32),
        ),
        name="attend_backward",
        compiler_params=pltpu.CompilerParams(vmem_limit_bytes=48 << 20),
    )(full, count, slots, q, do, k, v, jnp.broadcast_to(limits[None, :], (8, n)), lse, delta)


epsilon = 1e-05
gelu_coeff = 0.7978845608028654


def send(x, axis, mask):
    size = lax.axis_size(axis)
    return lax.ppermute(x, axis, [(i, i ^ mask) for i in range(size)])


def send_pair(x, i, j):
    count_row, count_col = lax.axis_size("row"), lax.axis_size("col")
    pairs = [
        (a * count_col + b, (a ^ i) * count_col + (b ^ j))
        for a in range(count_row)
        for b in range(count_col)
    ]
    return lax.ppermute(x, ("row", "col"), pairs)


def masks_of(axis):
    size = lax.axis_size(axis)
    return [1 << k for k in reversed(range(size.bit_length() - 1))]


def other_key(key, axis, mask):
    return (key[0] ^ mask, key[1]) if axis == "row" else (key[0], key[1] ^ mask)


def grow(parts, axis, masks):
    for mask in masks:
        parts = parts + [send(part, axis, mask) for part in parts]
    return parts


class Fold:
    def __init__(self, left, right):
        self.left, self.right, self.arrived = left, right, []
        self.limits = [left.shape[1], right.shape[1]]

    def part(self, rows, cols):
        made = dot_tn(self.left[:, rows[0] : rows[1]], self.right[:, cols[0] : cols[1]])
        for other in self.arrived:
            made = made + other[rows[0] : rows[1], cols[0] : cols[1]].astype(f32)
        return made

    def step(self, dim, axis, mask, *needed):
        if needed:
            self.left = after(self.left, *needed)
        half = self.limits[dim] // 2
        spans = [(0, self.limits[0]), (0, self.limits[1])]
        spans[dim] = (half, self.limits[dim])
        leaving = self.part(*spans).astype(bf16)
        self.arrived = [lax.slice_in_dim(other, 0, half, axis=dim) for other in self.arrived]
        self.arrived.append(send(leaving, axis, mask))
        self.limits[dim] = half
        return leaving

    def home(self, skip=0):
        kept = self.arrived
        self.arrived = kept[: len(kept) - skip]
        made = self.part((0, self.limits[0]), (0, self.limits[1]))
        self.arrived = kept
        return made


def halve_sum(x, steps):
    for axis, mask in steps:
        half = x.shape[0] // 2
        x = x[:half] + send(x[half:], axis, mask)
    return x


def after(x, *needed):
    return lax.optimization_barrier((x,) + needed)[0]


def everywhere(x, axes):
    for axis in axes:
        for mask in masks_of(axis):
            x = x + send(x, axis, mask)
    return x


def gelu_tanh(values):
    return (
        0.5 * values * (1.0 + jnp.tanh(gelu_coeff * (values + 0.044715 * values * values * values)))
    )


def gelu_slope(values):
    square = values * values
    curve = jnp.tanh(gelu_coeff * values * (1.0 + 0.044715 * square))
    return 0.5 * (1.0 + curve) + 0.5 * values * (1.0 - curve * curve) * gelu_coeff * (
        1.0 + 3.0 * 0.044715 * square
    )


def norm_forward(values, gain, shift):
    means = jnp.mean(values, 1, keepdims=True)
    squares = jnp.mean(values * values, 1, keepdims=True)
    inverse = lax.rsqrt(squares - means * means + epsilon)
    normal = (values - means) * inverse
    return (normal, inverse, (normal * gain + shift).astype(bf16))


def norm_backward(grad, normal, inverse, gain):
    scaled = grad * gain
    return inverse * (
        scaled
        - jnp.mean(scaled, 1, keepdims=True)
        - normal * jnp.mean(scaled * normal, 1, keepdims=True)
    )


def dot_nn(a, b):
    return lax.dot_general(a, b, NN, preferred_element_type=f32)


def dot_nt(a, b):
    return lax.dot_general(a, b, NT, preferred_element_type=f32)


def dot_tn(a, b):
    return lax.dot_general(a, b, TN, preferred_element_type=f32)


def flips():
    if lax.axis_size("row") == 2:
        return [lax.axis_index("row") ^ i for i in range(2)]
    return [0, 1]


def pick(halves, bit):
    rows = halves.shape[0] // 2
    return [
        lax.dynamic_slice_in_dim(halves, jnp.where(bit == stay, 0, rows), rows, 0)
        for stay in (0, 1)
    ]


def place_bits(mask):
    count_col = lax.axis_size("col")
    col = lax.axis_index("col")
    return [jnp.where((col ^ ((count_col - 1) * flip)) & mask, 1, 0) for flip in flips()]


def to_tokens_direct(block, chunk):
    count_row, count_col = lax.axis_size("row"), lax.axis_size("col")
    out = {}
    for i in range(2):
        for j in range(count_col):
            flip = lax.axis_index("row") if count_row == 2 else i
            place = lax.axis_index("col") ^ j ^ ((count_col - 1) * flip)
            part = lax.dynamic_slice_in_dim(block, (i * count_col + place) * chunk, chunk, 0)
            if count_row == 2:
                out[(i, j)] = send_pair(part, i, j) if i or j else part
            else:
                out[(i, j)] = send(part, "col", j) if j else part
    return out


def to_tokens(block, chunk, waits):
    half = block.shape[0] // 2
    lower, upper = block[:half], block[half:]
    if lax.axis_size("row") == 2:
        upper = send(after(upper, waits[0]), "row", 1)
    groups = {(0, 0): lower, (1, 0): upper}
    for mask, wait in zip(masks_of("col"), waits[1:]):
        groups[(1, 0)] = after(groups[(1, 0)], wait)
        bits = place_bits(mask)
        leaving = []
        for key in list(groups):
            groups[key], gone = pick(groups[key], bits[key[0]])
            leaving.append(gone)
        arrived = send(jnp.concatenate(leaving, 0), "col", mask)
        rows = leaving[0].shape[0]
        for k, key in enumerate(list(groups)):
            groups[(key[0], key[1] ^ mask)] = arrived[k * rows : (k + 1) * rows]
    return groups


def assemble(groups, order):
    return jnp.concatenate(
        [jnp.concatenate([groups[(i, j)] for j in order], 1) for i in range(2)], 0
    )


def from_tokens(tokens, chunk, width, order):
    low = tokens.astype(bf16)
    groups = {
        (i, j): low[i * chunk : (i + 1) * chunk, k * width : (k + 1) * width]
        for i in range(2)
        for k, j in enumerate(order)
    }
    for mask in masks_of("col")[::-1]:
        bits = place_bits(mask)
        leaving = [key for key in groups if key[1] & mask]
        rows = groups[leaving[0]].shape[0]
        arrived = send(jnp.concatenate([groups[key] for key in leaving], 0), "col", mask)
        for k, key in enumerate(leaving):
            del groups[key]
            kept = groups[(key[0], key[1] ^ mask)]
            came = arrived[k * rows : (k + 1) * rows]
            swap = bits[key[0]] == 1
            groups[(key[0], key[1] ^ mask)] = jnp.concatenate(
                [jnp.where(swap, came, kept), jnp.where(swap, kept, came)], 0
            )
    upper = groups[(1, 0)]
    if lax.axis_size("row") == 2:
        upper = send(upper, "row", 1)
    return jnp.concatenate([groups[(0, 0)], upper], 0).astype(f32)


def token_starts(chunk):
    count_row, count_col = lax.axis_size("row"), lax.axis_size("col")
    r, c = lax.axis_index("row"), lax.axis_index("col")
    if count_row == 2:
        own = r * count_col + c
        low, high = own * chunk, (4 * count_col - 1 - own) * chunk
        return [jnp.where(r == 0, low, high), jnp.where(r == 0, high, low)]
    return [(r * 2 * count_col + c) * chunk, (r * 2 * count_col + 2 * count_col - 1 - c) * chunk]


def key_slots():
    count_row, count_col = lax.axis_size("row"), lax.axis_size("col")
    r, c = lax.axis_index("row"), lax.axis_index("col")
    group = jnp.arange(2 * count_row * count_col, dtype=jnp.int32)
    half = group // (2 * count_col)
    if count_row == 2:
        owner = jnp.where(half == 0, group, 4 * count_col - 1 - group)
        owner_row, owner_col = owner // count_col, owner % count_col
        which = owner_row ^ half
    else:
        local = group % (2 * count_col)
        owner_row = half
        which = (local >= count_col).astype(jnp.int32)
        owner_col = jnp.where(which == 0, local, 2 * count_col - 1 - local)
    place = jnp.zeros_like(group)
    for k, (axis, mask) in enumerate(gather_steps()):
        relative = owner_row ^ r if axis == "row" else owner_col ^ c
        place = place + jnp.where(relative & mask, 1 << k, 0)
    return place * 2 + which


def gather_steps():
    col = [("col", mask) for mask in masks_of("col")]
    return col[:-1] + [("row", mask) for mask in masks_of("row")] + col[-1:]


def inward(total, wire):
    if lax.axis_size("dp") != 4:
        return total
    return lax.ppermute(total.astype(wire), "dp", [(0, 1), (3, 2)])


def across_middle(total, arrived, wire):
    if lax.axis_size("dp") != 4:
        return (total, total)
    held = (total + arrived.astype(f32)).astype(wire)
    return (held, lax.ppermute(held, "dp", [(1, 2), (2, 1)]))


def outward(held, arrived, wire):
    if lax.axis_size("dp") != 4:
        return everywhere(held, ["dp"])
    final = (held.astype(f32) + arrived.astype(f32)).astype(wire)
    z = lax.axis_index("dp")
    end = lax.ppermute(final, "dp", [(1, 0), (2, 3)])
    return jnp.where((z == 1) | (z == 2), final, end).astype(f32)


def per_device(
    layer_input,
    norm1_gain,
    norm1_shift,
    w_query,
    b_query,
    w_keyval,
    b_value,
    w_attn_out,
    b_attn_out,
    norm2_gain,
    norm2_shift,
    w_fc_in,
    b_fc_in,
    w_fc_out,
    b_fc_out,
    valid_mask,
    block_ids,
    teacher,
    out_cotangent,
):
    count_row = lax.axis_size("row")
    count_col = lax.axis_size("col")
    count_dp = lax.axis_size("dp")
    rows_a, width = layer_input.shape
    wide = w_query.shape[1]
    chunk = rows_a // (2 * count_col)
    col_far, near = masks_of("col")[:-1], masks_of("col")[-1]
    row_masks = masks_of("row")
    all_out = gather_steps()[::-1]
    order = [0]
    for mask in masks_of("col"):
        order = order + [j ^ mask for j in order]
    split = D // 2
    valid_flat = valid_mask.reshape(-1)
    block_flat = block_ids.reshape(-1)

    x_groups = to_tokens_direct(layer_input, chunk)
    keyval_near = jnp.concatenate(grow([w_keyval], "col", col_far), 0)
    keyval_far = send(keyval_near, "col", near)
    query_parts = [
        jnp.concatenate(parts, 0)
        for parts in zip(*[grow([part], "row", row_masks) for part in grow([w_query], "col", col_far)])
    ]
    query_near = jnp.concatenate(query_parts, 0)
    query_far = send(query_near, "col", near)
    vectors = jnp.stack(
        [norm1_gain, norm1_shift, b_attn_out, norm2_gain, norm2_shift, b_fc_out]
    )
    vectors = jnp.concatenate(grow([vectors], "col", col_far), 1)
    vectors = jnp.concatenate([vectors, send(vectors, "col", near)], 1)
    gain1, shift1, bias_o, gain2, shift2, bias_out = [vectors[k : k + 1] for k in range(6)]
    bias_q = jnp.concatenate(grow([b_query[None, :]], "row", row_masks), 1)

    starts = token_starts(chunk)
    block_own = jnp.concatenate(
        [lax.dynamic_slice_in_dim(block_flat, start, chunk, 0) for start in starts]
    )
    valid_own = jnp.concatenate(
        [lax.dynamic_slice_in_dim(valid_flat, start, chunk, 0) for start in starts]
    ).astype(f32)[:, None]
    valid_length = jnp.sum(valid_flat)
    reach = jnp.sum((block_flat[None, :] <= block_own[:, None]).astype(jnp.int32), 1)
    limits = jnp.minimum(reach, valid_length)
    slots = key_slots()

    residual = assemble(x_groups, order).astype(f32)
    normal1, inverse1, normed1 = norm_forward(residual, gain1, shift1)
    keyval = dot_nn(normed1[:, :split], keyval_near) + dot_nn(normed1[:, split:], keyval_far)
    keyval = jnp.concatenate(
        [keyval[:, :HEAD].astype(bf16), (keyval[:, HEAD:] + b_value).astype(bf16)], 1
    )
    keyval_far_rows = grow([keyval], "col", col_far)
    keyval_all = jnp.concatenate(keyval_far_rows, 0)
    keyval_all = jnp.concatenate(grow([keyval_all], "row", row_masks), 0)
    keyval_all = jnp.concatenate([keyval_all, send(keyval_all, "col", near)], 0)
    attn_cols = grow([after(w_attn_out, keyval_far_rows[-1])], "col", col_far)
    fc_in_rows = grow([after(w_fc_in, attn_cols[-1])], "col", col_far)
    keys, values = keyval_all[:, :HEAD], keyval_all[:, HEAD:]
    queries = jnp.concatenate(
        [
            dot_nn(normed1[:, :split], query_near[i * split : (i + 1) * split])
            + dot_nn(normed1[:, split:], query_far[i * split : (i + 1) * split])
            for i in range(count_row)
        ],
        1,
    )
    queries = (queries + bias_q).astype(bf16)
    attn_near = jnp.concatenate(
        grow([after(jnp.concatenate(attn_cols, 1), queries)], "row", row_masks), 0
    )
    attn_far = send(attn_near, "col", near)
    fc_out_cols = grow([after(w_fc_out, queries)], "col", col_far)
    attended, log_totals = attend_forward(queries, keys, values, limits, slots, chunk)
    middle = residual + (
        jnp.concatenate([dot_nn(attended, attn_near), dot_nn(attended, attn_far)], 1) + bias_o
    )
    normal2, inverse2, normed2 = norm_forward(middle, gain2, shift2)
    own = normed2.shape[0]
    fc_in_near = jnp.concatenate(fc_in_rows[:-1] + [after(fc_in_rows[-1], attended)], 0)
    fc_in_far = send(fc_in_near, "col", near)
    fc_out_near = jnp.concatenate(fc_out_cols, 1)
    fc_out_far = send(fc_out_near, "col", near)

    def col_product(x, first, second):
        return dot_nn(x[:, :split], first) + dot_nn(x[:, split:], second)

    def col_product_back(x, first, second):
        return dot_nt(x[:, :split], first) + dot_nt(x[:, split:], second)

    def row_gather(x):
        return jnp.concatenate(grow([x], "row", row_masks), 0)

    def row_sum(x):
        for mask in row_masks[::-1]:
            half = x.shape[0] // 2
            x = x[:half] + send(x[half:].astype(bf16), "row", mask).astype(f32)
        return x

    normed2_all = row_gather(normed2)
    pre_act = col_product(normed2_all, fc_in_near, fc_in_far) + b_fc_in
    act = gelu_tanh(pre_act).astype(bf16)
    fc_out_parts = jnp.concatenate([dot_nn(act, fc_out_near), dot_nn(act, fc_out_far)], 1)
    layer_output = middle + (row_sum(fc_out_parts) + bias_out)
    valid_count = jnp.full((8, 128), valid_length.astype(f32))
    valid_count = everywhere(after(valid_count, attended), ["dp"])[0, 0]
    late_groups = [
        to_tokens(block, chunk, [attended, normed2_all, act])
        for block in (teacher, out_cotangent)
    ]
    target = assemble(late_groups[0], order)
    cotangent = assemble(late_groups[1], order)
    errors = layer_output - target.astype(f32)
    loss_part = jnp.sum(valid_own * errors * errors)
    ratio = rows_a * count_row * count_dp / valid_count
    grad_out = cotangent.astype(f32) + ratio * valid_own * errors
    grad_mlp = grad_out.astype(bf16)
    grad_fc_out_bias = jnp.sum(grad_mlp, 0, dtype=f32)
    grad_mlp_all = row_gather(grad_mlp)
    output_block = from_tokens(after(layer_output, grad_mlp_all), chunk, width, order)

    parts = 2
    hidden = act.shape[1] // parts
    spans = [slice(f * hidden, (f + 1) * hidden) for f in range(parts)]
    out_folds = [Fold(act[:, span], grad_mlp_all) for span in spans]
    sent = []
    for mask in [near] + col_far[::-1]:
        for fold in out_folds:
            sent = [fold.step(1, "col", mask, *sent)]
    grad_pre = (
        col_product_back(after(grad_mlp_all, *sent), fc_out_near, fc_out_far)
        * gelu_slope(pre_act)
    ).astype(bf16)
    grad_fc_in_bias = jnp.sum(grad_pre, 0, dtype=f32)
    homes = [fold.home(1) for fold in out_folds]
    total_0 = homes[0] + out_folds[0].arrived[-1].astype(f32)
    low_0 = total_0.astype(bf16)
    grad_pre = after(grad_pre, low_0, homes[1])
    normed2_grads = jnp.concatenate([dot_nt(grad_pre, fc_in_near), dot_nt(grad_pre, fc_in_far)], 1)
    leaving = normed2_grads[own * count_row // 2 :].astype(bf16)
    arrived = send(leaving, "row", row_masks[-1])
    in_folds = [Fold(normed2_all, grad_pre[:, span]) for span in spans]
    sent = [in_folds[0].step(0, "col", near, leaving)]
    total_1 = homes[1] + after(out_folds[1].arrived[-1], *sent).astype(f32)
    low_1 = total_1.astype(bf16)
    sent = [in_folds[1].step(0, "col", near, low_1)]
    for mask in col_far[::-1]:
        for fold in in_folds:
            sent = [fold.step(0, "col", mask, *sent)]
    homes_in = [fold.home(1) for fold in in_folds]
    grad_normed2 = normed2_grads[: own * count_row // 2] + after(
        arrived, *sent, *homes_in
    ).astype(f32)
    for mask in row_masks[:-1][::-1]:
        half = grad_normed2.shape[0] // 2
        grad_normed2 = grad_normed2[:half] + send(
            grad_normed2[half:].astype(bf16), "row", mask
        ).astype(f32)

    gain2_part = jnp.sum(grad_normed2 * normal2, 0)
    shift2_part = jnp.sum(grad_normed2, 0)
    grad_middle = grad_out + norm_backward(grad_normed2, normal2, inverse2, gain2)
    grad_attn = grad_middle.astype(bf16)
    grad_attn_bias = jnp.sum(grad_attn, 0, dtype=f32)
    low_2 = (homes_in[0] + in_folds[0].arrived[-1].astype(f32)).astype(bf16)
    sum_0, sum_1 = lax.psum((low_0, low_1), "dp")

    attn_fold = Fold(attended, after(grad_attn, low_2))
    sent = attn_fold.step(1, "col", near)
    grad_attended = col_product_back(after(grad_attn, sent), attn_near, attn_far).astype(bf16)
    for mask in row_masks[::-1]:
        sent = attn_fold.step(0, "row", mask, sent)

    heads = queries.shape[1] // HEAD
    delta = jnp.sum(
        (attended.astype(f32) * grad_attended.astype(f32)).reshape(own, heads, HEAD), -1
    ).T
    grad_queries, grad_keys, grad_values = attend_backward(
        queries,
        after(grad_attended, low_2),
        keys,
        values,
        limits,
        slots,
        log_totals,
        delta,
        chunk,
    )
    grad_keyval = jnp.concatenate([grad_keys, grad_values], 1)
    low_3 = homes_in[1] + after(in_folds[1].arrived[-1], grad_queries).astype(f32)
    low_3 = low_3.astype(bf16)
    low_2, low_3 = lax.optimization_barrier((low_2, low_3, sum_0, sum_1))[:2]
    sum_2, sum_3 = lax.psum((low_2, low_3), "dp")
    grad_keyval_low = halve_sum(grad_keyval, all_out).astype(bf16)

    query_fold = Fold(normed1, grad_queries)
    sent = query_fold.step(0, "col", near)
    for mask in col_far[::-1]:
        sent_attn = attn_fold.step(1, "col", mask, sent)
    query_grads = jnp.concatenate([
        sum(
            dot_nt(
                after(grad_queries, sent, sent_attn)[:, i * wide : (i + 1) * wide],
                weights[i * split : (i + 1) * split],
            )
            for i in range(count_row)
        )
        for weights in (query_near, query_far)
    ], 1)
    for mask in row_masks[::-1]:
        sent = query_fold.step(1, "row", mask, sent)
    total_4 = attn_fold.home()
    in_4 = inward(total_4.astype(bf16), bf16)
    grad_value_bias = jnp.sum(grad_keyval_low[:, HEAD:], 0, dtype=f32)
    grad_query_bias = jnp.sum(grad_queries, 0, dtype=f32)
    for mask in col_far[::-1]:
        sent = query_fold.step(0, "col", mask, sent)

    grad_keyval_w = everywhere(
        halve_sum(dot_tn(normed1, grad_keyval_low), [step for step in all_out if step[0] == "col"]),
        ["row", "dp"],
    )
    grad_normed1 = query_grads + jnp.concatenate(
        [dot_nt(grad_keyval_low, keyval_near), dot_nt(grad_keyval_low, keyval_far)], 1
    )
    gain1_part = jnp.sum(grad_normed1 * normal1, 0)
    shift1_part = jnp.sum(grad_normed1, 0)
    input_grad = grad_middle + norm_backward(grad_normed1, normal1, inverse1, gain1)
    input_block = from_tokens(input_grad, chunk, width, order)

    held_4, mid_4 = across_middle(total_4, in_4, bf16)
    total_5 = query_fold.home()
    in_5 = inward(total_5.astype(bf16), bf16)
    grad_attn_out = outward(held_4, mid_4, bf16)
    held_5, mid_5 = across_middle(total_5, in_5, bf16)
    grad_query_w = outward(held_5, mid_5, bf16)
    grad_fc_out = jnp.concatenate([sum_0, sum_1], 0).astype(f32)
    grad_fc_in = jnp.concatenate([sum_2, sum_3], 1).astype(f32)

    unit = min(width, wide)
    per = width // unit
    feature_rows = jnp.stack(
        [gain1_part, shift1_part, gain2_part, shift2_part, grad_fc_out_bias, grad_attn_bias]
    )
    tail = jnp.concatenate([grad_value_bias, loss_part[None], jnp.zeros((unit - HEAD - 1,), f32)])
    shared = jnp.concatenate([tail, grad_query_bias, grad_fc_in_bias]).reshape(-1, unit)
    features = feature_rows.reshape(6, count_col, per, unit).transpose(1, 0, 2, 3)
    features = features.reshape(-1, unit)
    for mask in masks_of("col")[::-1]:
        half = features.shape[0] // 2
        came = send(jnp.concatenate([features[half:], shared], 0), "col", mask)
        features = features[:half] + came[:half]
        shared = shared + came[half:]
    ahead, each = 6 * per + 1, wide // unit
    pack = jnp.concatenate([features, shared], 0)
    query_sum = halve_sum(
        pack[ahead : ahead + count_row * each], [("row", mask) for mask in row_masks[::-1]]
    )
    hidden_rows = pack[ahead + count_row * each :]
    pack = jnp.concatenate([everywhere(pack[:ahead], ["row"]), query_sum, hidden_rows], 0)
    pack = everywhere(pack, ["dp"])
    vector_sums = [pack[k * per : (k + 1) * per].reshape(-1) for k in range(6)]
    value_bias_sum = pack[6 * per, :HEAD]
    loss_sum = pack[6 * per, HEAD]
    query_bias_sum = pack[ahead : ahead + each].reshape(-1)
    fc_in_bias_sum = pack[ahead + each :].reshape(-1)
    return (
        output_block,
        loss_sum / (valid_count * D),
        input_block,
        vector_sums[0],
        vector_sums[1],
        grad_query_w,
        query_bias_sum,
        grad_keyval_w,
        value_bias_sum,
        grad_attn_out,
        vector_sums[5],
        vector_sums[2],
        vector_sums[3],
        grad_fc_in,
        fc_in_bias_sum,
        grad_fc_out,
        vector_sums[4],
    )


def solution(mesh):
    placed = (
        P(("dp", "row"), "col"),
        P("col"),
        P("col"),
        P("col", "row"),
        P("row"),
        P("col", None),
        P(),
        P("row", "col"),
        P("col"),
        P("col"),
        P("col"),
        P("col", "row"),
        P("row"),
        P("row", "col"),
        P("col"),
        P("dp", None),
        P("dp", None),
        P(("dp", "row"), "col"),
        P(("dp", "row"), "col"),
    )
    return jax.shard_map(
        per_device,
        mesh=mesh,
        in_specs=placed,
        out_specs=(
            P(("dp", "row"), "col"),
            P(),
            P(("dp", "row"), "col"),
            P("col"),
            P("col"),
            P("col", "row"),
            P("row"),
            P("col", None),
            P(),
            P("row", "col"),
            P("col"),
            P("col"),
            P("col"),
            P("col", "row"),
            P("row"),
            P("row", "col"),
            P("col"),
        ),
        check_vma=False,
    )
```

```python
import functools
import jax, jax.numpy as jnp
from jax import lax
from jax.experimental import pallas as pl
from jax.experimental.pallas import tpu as pltpu
from jax.sharding import PartitionSpec as P

D = 2048
HEAD = 128
SCALE = HEAD**-0.5
SC = SCALE * 1.4426950408889634
NT = (((1,), (1,)), ((), ()))
NN = (((1,), (0,)), ((), ()))
TN = (((0,), (0,)), ((), ()))
f32 = jnp.float32
bf16 = jnp.bfloat16


def stack_heads(ref, heads):
    return jnp.concatenate([ref[:, h * HEAD : (h + 1) * HEAD] for h in range(heads)], axis=0)


def key_rows(ref, slot_ref, block, per_block, chunk):
    parts = [
        ref[pl.ds(pl.multiple_of(slot_ref[block * per_block + s] * chunk, chunk), chunk), :]
        for s in range(per_block)
    ]
    return parts[0] if per_block == 1 else jnp.concatenate(parts, axis=0)


def fwd_kernel(
    full_ref, count_ref, slot_ref, q_ref, k_ref, v_ref, lim_ref, o_ref, lse_ref, acc, top, tot,
    *, heads, tq, chunk, per_block
):
    t = pl.program_id(0)
    bk = chunk * per_block
    q = stack_heads(q_ref, heads)
    acc[...] = jnp.zeros_like(acc)
    top[...] = jnp.full_like(top, -1e30)
    tot[...] = jnp.zeros_like(tot)

    def step(block, masked):
        kk = key_rows(k_ref, slot_ref, block, per_block, chunk)
        vv = key_rows(v_ref, slot_ref, block, per_block, chunk)
        s = lax.dot_general(kk, q, NT, preferred_element_type=f32)
        if masked:
            ids = lax.broadcasted_iota(jnp.int32, (bk, heads * tq), 0) + block * bk
            lim = jnp.concatenate([lim_ref[:1, :]] * heads, axis=1)
            s = jnp.where(ids < lim, s, -1e30)
        before = top[...]
        now = jnp.maximum(before, jnp.max(s, axis=0, keepdims=True))
        p = jnp.exp2(s * SC - now * SC)
        top[...] = now
        a = jnp.exp2((before - now) * SC)
        tot[...] = tot[...] * a + jnp.sum(p, axis=0, keepdims=True)
        acc[...] = acc[...] * a + lax.dot_general(
            vv, p.astype(bf16), TN, preferred_element_type=f32
        )

    lax.fori_loop(0, full_ref[t], lambda b, c: (step(b, False), c)[1], 0)
    lax.fori_loop(full_ref[t], count_ref[t], lambda b, c: (step(b, True), c)[1], 0)
    o = acc[...] * (1.0 / tot[...])
    lse = top[...] * SC + jnp.log2(tot[...])
    for h in range(heads):
        o_ref[:, h * HEAD : (h + 1) * HEAD] = jnp.transpose(o[:, h * tq : (h + 1) * tq]).astype(bf16)
        lse_ref[h : h + 1, :] = lse[:, h * tq : (h + 1) * tq]


def bwd_kernel(
    full_ref, count_ref, slot_ref, q_ref, do_ref, k_ref, v_ref, lim_ref, lse_ref, dl_ref,
    dq_ref, dk_ref, dv_ref, dqa, *, heads, tq, chunk, per_block
):
    t = pl.program_id(0)
    bk = chunk * per_block

    @pl.when((t == 0) & (pl.program_id(1) == 0))
    def _():
        dk_ref[...] = jnp.zeros_like(dk_ref)
        dv_ref[...] = jnp.zeros_like(dv_ref)

    q = stack_heads(q_ref, heads)
    do = stack_heads(do_ref, heads)
    lse = jnp.concatenate([lse_ref[h : h + 1, :] for h in range(heads)], axis=1)
    dl = jnp.concatenate([dl_ref[h : h + 1, :] for h in range(heads)], axis=1)
    dqa[...] = jnp.zeros_like(dqa)

    def step(block, masked):
        kk = key_rows(k_ref, slot_ref, block, per_block, chunk)
        vv = key_rows(v_ref, slot_ref, block, per_block, chunk)
        s = lax.dot_general(kk, q, NT, preferred_element_type=f32)
        p = jnp.exp2(s * SC - lse)
        if masked:
            ids = lax.broadcasted_iota(jnp.int32, (bk, heads * tq), 0) + block * bk
            lim = jnp.concatenate([lim_ref[:1, :]] * heads, axis=1)
            p = jnp.where(ids < lim, p, 0.0)
        dp = lax.dot_general(vv, do, NT, preferred_element_type=f32)
        ds = (p * (dp - dl)).astype(bf16)
        dv = lax.dot_general(p.astype(bf16), do, NN, preferred_element_type=f32)
        dk = lax.dot_general(ds, q, NN, preferred_element_type=f32)
        dqa[...] += lax.dot_general(ds, kk, TN, preferred_element_type=f32)
        for s in range(per_block):
            off = pl.multiple_of(slot_ref[block * per_block + s] * chunk, chunk)
            dk_ref[pl.ds(off, chunk), :] += dk[s * chunk : (s + 1) * chunk]
            dv_ref[pl.ds(off, chunk), :] += dv[s * chunk : (s + 1) * chunk]

    lax.fori_loop(0, full_ref[t], lambda b, c: (step(b, False), c)[1], 0)
    lax.fori_loop(full_ref[t], count_ref[t], lambda b, c: (step(b, True), c)[1], 0)
    dq = (dqa[...] * HEAD**-0.5).astype(bf16)
    for h in range(heads):
        dq_ref[:, h * HEAD : (h + 1) * HEAD] = dq[h * tq : (h + 1) * tq]

    @pl.when((t == pl.num_programs(0) - 1) & (pl.program_id(1) == pl.num_programs(1) - 1))
    def _():
        dk_ref[...] = dk_ref[...] * HEAD**-0.5


def block_counts(limits, tq, bk):
    tiles = limits.reshape(-1, tq)
    return jnp.min(tiles, 1) // bk, (jnp.max(tiles, 1) + bk - 1) // bk


def attend_forward(q, k, v, limits, slots, chunk, tq=128, heads=16, bk=256):
    n, hq = q.shape
    total = hq // HEAD
    per_block = max(1, bk // chunk)
    full, count = block_counts(limits, tq, chunk * per_block)
    rows = k.shape[0]
    grid = pltpu.PrefetchScalarGridSpec(
        num_scalar_prefetch=3,
        grid=(n // tq, total // heads),
        in_specs=[
            pl.BlockSpec((tq, heads * HEAD), lambda t, g, *_: (t, g)),
            pl.BlockSpec((rows, HEAD), lambda t, g, *_: (0, 0)),
            pl.BlockSpec((rows, HEAD), lambda t, g, *_: (0, 0)),
            pl.BlockSpec((8, tq), lambda t, g, *_: (0, t)),
        ],
        out_specs=[
            pl.BlockSpec((tq, heads * HEAD), lambda t, g, *_: (t, g)),
            pl.BlockSpec((heads, tq), lambda t, g, *_: (g, t)),
        ],
        scratch_shapes=[
            pltpu.VMEM((HEAD, heads * tq), f32),
            pltpu.VMEM((1, heads * tq), f32),
            pltpu.VMEM((1, heads * tq), f32),
        ],
    )
    return pl.pallas_call(
        functools.partial(fwd_kernel, heads=heads, tq=tq, chunk=chunk, per_block=per_block),
        grid_spec=grid,
        out_shape=(jax.ShapeDtypeStruct((n, hq), bf16), jax.ShapeDtypeStruct((total, n), f32)),
        name="attend_forward",
        compiler_params=pltpu.CompilerParams(vmem_limit_bytes=48 << 20),
    )(full, count, slots, q, k, v, jnp.broadcast_to(limits[None, :], (8, n)))


def attend_backward(q, do, k, v, limits, slots, lse, delta, chunk, tq=128, heads=16, bk=256):
    n, hq = q.shape
    total = hq // HEAD
    per_block = max(1, bk // chunk)
    full, count = block_counts(limits, tq, chunk * per_block)
    rows = k.shape[0]
    token_block = pl.BlockSpec((tq, heads * HEAD), lambda t, g, *_: (t, g))
    key_block = pl.BlockSpec((rows, HEAD), lambda t, g, *_: (0, 0))
    head_block = pl.BlockSpec((heads, tq), lambda t, g, *_: (g, t))
    grid = pltpu.PrefetchScalarGridSpec(
        num_scalar_prefetch=3,
        grid=(n // tq, total // heads),
        in_specs=[
            token_block, token_block, key_block, key_block,
            pl.BlockSpec((8, tq), lambda t, g, *_: (0, t)),
            head_block, head_block,
        ],
        out_specs=[token_block, key_block, key_block],
        scratch_shapes=[pltpu.VMEM((heads * tq, HEAD), f32)],
    )
    return pl.pallas_call(
        functools.partial(bwd_kernel, heads=heads, tq=tq, chunk=chunk, per_block=per_block),
        grid_spec=grid,
        out_shape=(
            jax.ShapeDtypeStruct((n, hq), bf16),
            jax.ShapeDtypeStruct((rows, HEAD), f32),
            jax.ShapeDtypeStruct((rows, HEAD), f32),
        ),
        name="attend_backward",
        compiler_params=pltpu.CompilerParams(vmem_limit_bytes=48 << 20),
    )(full, count, slots, q, do, k, v, jnp.broadcast_to(limits[None, :], (8, n)), lse, delta)


epsilon = 1e-05
gelu_coeff = 0.7978845608028654


def send(x, axis, mask):
    size = lax.axis_size(axis)
    return lax.ppermute(x, axis, [(i, i ^ mask) for i in range(size)])


def send_pair(x, i, j):
    count_row, count_col = lax.axis_size("row"), lax.axis_size("col")
    pairs = [
        (a * count_col + b, (a ^ i) * count_col + (b ^ j))
        for a in range(count_row)
        for b in range(count_col)
    ]
    return lax.ppermute(x, ("row", "col"), pairs)


def masks_of(axis):
    size = lax.axis_size(axis)
    return [1 << k for k in reversed(range(size.bit_length() - 1))]


def other_key(key, axis, mask):
    return (key[0] ^ mask, key[1]) if axis == "row" else (key[0], key[1] ^ mask)


def grow(parts, axis, masks):
    for mask in masks:
        parts = parts + [send(part, axis, mask) for part in parts]
    return parts


def product_kernel(*refs):
    left, right, *others, out = refs
    made = lax.dot_general(left[...], right[...], TN, preferred_element_type=f32)
    for other in others:
        made = made + other[...].astype(f32)
    out[...] = made.astype(out.dtype)


def token_product(left, right, rows, cols, base, others, kind):
    tokens = left.shape[0]
    tall, broad = min(512, rows[1] - rows[0]), min(1024, cols[1] - cols[0])
    left_at, right_at = (base[0] + rows[0]) // tall, (base[1] + cols[0]) // broad
    row_at, col_at = rows[0] // tall, cols[0] // broad
    return pl.pallas_call(
        product_kernel,
        grid=((rows[1] - rows[0]) // tall, (cols[1] - cols[0]) // broad),
        in_specs=[
            pl.BlockSpec((tokens, tall), lambda i, j: (0, left_at + i)),
            pl.BlockSpec((tokens, broad), lambda i, j: (0, right_at + j)),
        ]
        + [pl.BlockSpec((tall, broad), lambda i, j: (row_at + i, col_at + j)) for _ in others],
        out_specs=pl.BlockSpec((tall, broad), lambda i, j: (i, j)),
        out_shape=jax.ShapeDtypeStruct((rows[1] - rows[0], cols[1] - cols[0]), kind),
        name="token_product",
        compiler_params=pltpu.CompilerParams(vmem_limit_bytes=48 << 20),
    )(left, right, *others)


class Fold:
    def __init__(self, left, right, base=(0, 0), size=None):
        self.left, self.right, self.base, self.arrived = left, right, base, []
        self.limits = list(size or (left.shape[1], right.shape[1]))

    def part(self, rows, cols, kind):
        return token_product(self.left, self.right, rows, cols, self.base, self.arrived, kind)

    def step(self, dim, axis, mask, *needed):
        if needed:
            self.left = after(self.left, *needed)
        half = self.limits[dim] // 2
        spans = [(0, self.limits[0]), (0, self.limits[1])]
        spans[dim] = (half, self.limits[dim])
        leaving = self.part(*spans, bf16)
        self.arrived = self.arrived + [send(leaving, axis, mask)]
        self.limits[dim] = half
        return leaving

    def home(self, skip=0):
        kept = self.arrived
        self.arrived = kept[: len(kept) - skip]
        made = self.part((0, self.limits[0]), (0, self.limits[1]), f32)
        self.arrived = kept
        return made


def halve_sum(x, steps):
    for axis, mask in steps:
        half = x.shape[0] // 2
        x = x[:half] + send(x[half:], axis, mask)
    return x


def after(x, *needed):
    return lax.optimization_barrier((x,) + needed)[0]


def everywhere(x, axes):
    for axis in axes:
        for mask in masks_of(axis):
            x = x + send(x, axis, mask)
    return x


def gelu_tanh(values):
    return (
        0.5 * values * (1.0 + jnp.tanh(gelu_coeff * (values + 0.044715 * values * values * values)))
    )


def gelu_slope(values):
    square = values * values
    curve = jnp.tanh(gelu_coeff * values * (1.0 + 0.044715 * square))
    return 0.5 * (1.0 + curve) + 0.5 * values * (1.0 - curve * curve) * gelu_coeff * (
        1.0 + 3.0 * 0.044715 * square
    )


def norm_forward(values, gain, shift):
    means = jnp.mean(values, 1, keepdims=True)
    squares = jnp.mean(values * values, 1, keepdims=True)
    inverse = lax.rsqrt(squares - means * means + epsilon)
    normal = (values - means) * inverse
    return (normal, inverse, (normal * gain + shift).astype(bf16))


def norm_backward(grad, normal, inverse, gain):
    scaled = grad * gain
    return inverse * (
        scaled
        - jnp.mean(scaled, 1, keepdims=True)
        - normal * jnp.mean(scaled * normal, 1, keepdims=True)
    )


def dot_nn(a, b):
    return lax.dot_general(a, b, NN, preferred_element_type=f32)


def dot_nt(a, b):
    return lax.dot_general(a, b, NT, preferred_element_type=f32)


def dot_tn(a, b):
    return lax.dot_general(a, b, TN, preferred_element_type=f32)


def flips():
    if lax.axis_size("row") == 2:
        return [lax.axis_index("row") ^ i for i in range(2)]
    return [0, 1]


def pick(halves, bit):
    rows = halves.shape[0] // 2
    return [
        lax.dynamic_slice_in_dim(halves, jnp.where(bit == stay, 0, rows), rows, 0)
        for stay in (0, 1)
    ]


def place_bits(mask):
    count_col = lax.axis_size("col")
    col = lax.axis_index("col")
    return [jnp.where((col ^ ((count_col - 1) * flip)) & mask, 1, 0) for flip in flips()]


def to_tokens_direct(block, chunk):
    count_row, count_col = lax.axis_size("row"), lax.axis_size("col")
    out = {}
    for i in range(2):
        for j in range(count_col):
            flip = lax.axis_index("row") if count_row == 2 else i
            place = lax.axis_index("col") ^ j ^ ((count_col - 1) * flip)
            part = lax.dynamic_slice_in_dim(block, (i * count_col + place) * chunk, chunk, 0)
            if count_row == 2:
                out[(i, j)] = send_pair(part, i, j) if i or j else part
            else:
                out[(i, j)] = send(part, "col", j) if j else part
    return out


def to_tokens(block, chunk, waits):
    half = block.shape[0] // 2
    lower, upper = block[:half], block[half:]
    if lax.axis_size("row") == 2:
        upper = send(after(upper, waits[0]), "row", 1)
    groups = {(0, 0): lower, (1, 0): upper}
    for mask, wait in zip(masks_of("col"), waits[1:]):
        groups[(1, 0)] = after(groups[(1, 0)], wait)
        bits = place_bits(mask)
        leaving = []
        for key in list(groups):
            groups[key], gone = pick(groups[key], bits[key[0]])
            leaving.append(gone)
        arrived = send(jnp.concatenate(leaving, 0), "col", mask)
        rows = leaving[0].shape[0]
        for k, key in enumerate(list(groups)):
            groups[(key[0], key[1] ^ mask)] = arrived[k * rows : (k + 1) * rows]
    return groups


def assemble(groups, order):
    return jnp.concatenate(
        [jnp.concatenate([groups[(i, j)] for j in order], 1) for i in range(2)], 0
    )


def from_tokens(tokens, chunk, width, order):
    low = tokens.astype(bf16)
    groups = {
        (i, j): low[i * chunk : (i + 1) * chunk, k * width : (k + 1) * width]
        for i in range(2)
        for k, j in enumerate(order)
    }
    for mask in masks_of("col")[::-1]:
        bits = place_bits(mask)
        leaving = [key for key in groups if key[1] & mask]
        rows = groups[leaving[0]].shape[0]
        arrived = send(jnp.concatenate([groups[key] for key in leaving], 0), "col", mask)
        for k, key in enumerate(leaving):
            del groups[key]
            kept = groups[(key[0], key[1] ^ mask)]
            came = arrived[k * rows : (k + 1) * rows]
            swap = bits[key[0]] == 1
            groups[(key[0], key[1] ^ mask)] = jnp.concatenate(
                [jnp.where(swap, came, kept), jnp.where(swap, kept, came)], 0
            )
    upper = groups[(1, 0)]
    if lax.axis_size("row") == 2:
        upper = send(upper, "row", 1)
    return jnp.concatenate([groups[(0, 0)], upper], 0).astype(f32)


def token_starts(chunk):
    count_row, count_col = lax.axis_size("row"), lax.axis_size("col")
    r, c = lax.axis_index("row"), lax.axis_index("col")
    if count_row == 2:
        own = r * count_col + c
        low, high = own * chunk, (4 * count_col - 1 - own) * chunk
        return [jnp.where(r == 0, low, high), jnp.where(r == 0, high, low)]
    return [(r * 2 * count_col + c) * chunk, (r * 2 * count_col + 2 * count_col - 1 - c) * chunk]


def key_slots():
    count_row, count_col = lax.axis_size("row"), lax.axis_size("col")
    r, c = lax.axis_index("row"), lax.axis_index("col")
    group = jnp.arange(2 * count_row * count_col, dtype=jnp.int32)
    half = group // (2 * count_col)
    if count_row == 2:
        owner = jnp.where(half == 0, group, 4 * count_col - 1 - group)
        owner_row, owner_col = owner // count_col, owner % count_col
        which = owner_row ^ half
    else:
        local = group % (2 * count_col)
        owner_row = half
        which = (local >= count_col).astype(jnp.int32)
        owner_col = jnp.where(which == 0, local, 2 * count_col - 1 - local)
    place = jnp.zeros_like(group)
    for k, (axis, mask) in enumerate(gather_steps()):
        relative = owner_row ^ r if axis == "row" else owner_col ^ c
        place = place + jnp.where(relative & mask, 1 << k, 0)
    return place * 2 + which


def gather_steps():
    col = [("col", mask) for mask in masks_of("col")]
    return col[:-1] + [("row", mask) for mask in masks_of("row")] + col[-1:]


def inward(total, wire):
    if lax.axis_size("dp") != 4:
        return total
    return lax.ppermute(total.astype(wire), "dp", [(0, 1), (3, 2)])


def across_middle(total, arrived, wire):
    if lax.axis_size("dp") != 4:
        return (total, total)
    held = (total + arrived.astype(f32)).astype(wire)
    return (held, lax.ppermute(held, "dp", [(1, 2), (2, 1)]))


def outward(held, arrived, wire):
    if lax.axis_size("dp") != 4:
        final = everywhere(held.astype(f32), ["dp"])
        return (final, final)
    final = (held.astype(f32) + arrived.astype(f32)).astype(wire)
    return (final, lax.ppermute(final, "dp", [(1, 0), (2, 3)]))


def settled(pair):
    final, end = pair
    if lax.axis_size("dp") != 4:
        return final
    z = lax.axis_index("dp")
    return jnp.where((z == 1) | (z == 2), final, end).astype(f32)


def per_device(
    layer_input,
    norm1_gain,
    norm1_shift,
    w_query,
    b_query,
    w_keyval,
    b_value,
    w_attn_out,
    b_attn_out,
    norm2_gain,
    norm2_shift,
    w_fc_in,
    b_fc_in,
    w_fc_out,
    b_fc_out,
    valid_mask,
    block_ids,
    teacher,
    out_cotangent,
):
    count_row = lax.axis_size("row")
    count_col = lax.axis_size("col")
    count_dp = lax.axis_size("dp")
    rows_a, width = layer_input.shape
    wide = w_query.shape[1]
    chunk = rows_a // (2 * count_col)
    col_far, near = masks_of("col")[:-1], masks_of("col")[-1]
    row_masks = masks_of("row")
    all_out = gather_steps()[::-1]
    order = [0]
    for mask in masks_of("col"):
        order = order + [j ^ mask for j in order]
    split = D // 2
    valid_flat = valid_mask.reshape(-1)
    block_flat = block_ids.reshape(-1)

    x_groups = to_tokens_direct(layer_input, chunk)
    keyval_near = jnp.concatenate(grow([w_keyval], "col", col_far), 0)
    keyval_far = send(keyval_near, "col", near)
    query_parts = [
        jnp.concatenate(parts, 0)
        for parts in zip(
            *[
                grow([part], "row", row_masks)
                for part in grow([after(w_query, *x_groups.values())], "col", col_far)
            ]
        )
    ]
    query_near = jnp.concatenate(query_parts, 0)
    query_far = send(query_near, "col", near)
    vectors = jnp.stack(
        [norm1_gain, norm1_shift, b_attn_out, norm2_gain, norm2_shift, b_fc_out]
    )
    vectors = jnp.concatenate(grow([vectors], "col", col_far), 1)
    vectors = jnp.concatenate([vectors, send(vectors, "col", near)], 1)
    gain1, shift1, bias_o, gain2, shift2, bias_out = [vectors[k : k + 1] for k in range(6)]
    bias_q = jnp.concatenate(grow([b_query[None, :]], "row", row_masks), 1)

    starts = token_starts(chunk)
    block_own = jnp.concatenate(
        [lax.dynamic_slice_in_dim(block_flat, start, chunk, 0) for start in starts]
    )
    valid_own = jnp.concatenate(
        [lax.dynamic_slice_in_dim(valid_flat, start, chunk, 0) for start in starts]
    ).astype(f32)[:, None]
    valid_length = jnp.sum(valid_flat)
    reach = jnp.sum((block_flat[None, :] <= block_own[:, None]).astype(jnp.int32), 1)
    limits = jnp.minimum(reach, valid_length)
    slots = key_slots()

    residual = assemble(x_groups, order).astype(f32)
    normal1, inverse1, normed1 = norm_forward(residual, gain1, shift1)
    keyval = dot_nn(normed1[:, :split], keyval_near) + dot_nn(normed1[:, split:], keyval_far)
    keyval = jnp.concatenate(
        [keyval[:, :HEAD].astype(bf16), (keyval[:, HEAD:] + b_value).astype(bf16)], 1
    )
    keyval_far_rows = grow([keyval], "col", col_far)
    keyval_all = jnp.concatenate(keyval_far_rows, 0)
    keyval_all = jnp.concatenate(grow([keyval_all], "row", row_masks), 0)
    keyval_all = jnp.concatenate([keyval_all, send(keyval_all, "col", near)], 0)
    attn_cols = grow([after(w_attn_out, keyval_far_rows[-1])], "col", col_far)
    fc_in_rows = grow([after(w_fc_in, attn_cols[-1])], "col", col_far)
    keys, values = keyval_all[:, :HEAD], keyval_all[:, HEAD:]
    queries = jnp.concatenate(
        [
            dot_nn(normed1[:, :split], query_near[i * split : (i + 1) * split])
            + dot_nn(normed1[:, split:], query_far[i * split : (i + 1) * split])
            for i in range(count_row)
        ],
        1,
    )
    queries = (queries + bias_q).astype(bf16)
    attn_rows = grow([after(jnp.concatenate(attn_cols, 1), queries)], "row", row_masks)
    fc_out_cols = grow([after(w_fc_out, queries)], "col", col_far)
    attended, log_totals = attend_forward(queries, keys, values, limits, slots, chunk)
    attn_near = jnp.concatenate(attn_rows[:-1] + [after(attn_rows[-1], attended)], 0)
    attn_far = send(attn_near, "col", near)
    middle = residual + (
        jnp.concatenate([dot_nn(attended, attn_near), dot_nn(attended, attn_far)], 1) + bias_o
    )
    normal2, inverse2, normed2 = norm_forward(middle, gain2, shift2)
    own = normed2.shape[0]
    fc_in_near = jnp.concatenate(fc_in_rows[:-1] + [after(fc_in_rows[-1], attended)], 0)
    fc_in_far = send(fc_in_near, "col", near)

    def col_product(x, first, second):
        return dot_nn(x[:, :split], first) + dot_nn(x[:, split:], second)

    def col_product_back(x, first, second):
        return dot_nt(x[:, :split], first) + dot_nt(x[:, split:], second)

    def row_gather(x):
        return jnp.concatenate(grow([x], "row", row_masks), 0)

    def row_sum(x):
        for mask in row_masks[::-1]:
            half = x.shape[0] // 2
            x = x[:half] + send(x[half:].astype(bf16), "row", mask).astype(f32)
        return x

    normed2_all = row_gather(normed2)
    pre_act = col_product(normed2_all, fc_in_near, fc_in_far) + b_fc_in
    act = gelu_tanh(pre_act).astype(bf16)
    fc_out_near = jnp.concatenate(fc_out_cols[:-1] + [after(fc_out_cols[-1], act)], 1)
    fc_out_far = send(fc_out_near, "col", near)
    fc_out_first = dot_nn(act, fc_out_near)
    fc_out_parts = jnp.concatenate([fc_out_first, dot_nn(act, fc_out_far)], 1)
    fc_out_sum = row_sum(fc_out_parts)
    layer_output = middle + (fc_out_sum + bias_out)
    valid_count = jnp.full((8, 128), valid_length.astype(f32))
    valid_count = everywhere(after(valid_count, attended), ["dp"])[0, 0]
    late_groups = [
        to_tokens(block, chunk, [act, fc_out_first, fc_out_sum])
        for block in (teacher, out_cotangent)
    ]
    target = assemble(late_groups[0], order)
    cotangent = assemble(late_groups[1], order)
    errors = layer_output - target.astype(f32)
    loss_part = jnp.sum(valid_own * errors * errors)
    ratio = rows_a * count_row * count_dp / valid_count
    grad_out = cotangent.astype(f32) + ratio * valid_own * errors
    grad_mlp = grad_out.astype(bf16)
    grad_fc_out_bias = jnp.sum(grad_mlp, 0, dtype=f32)
    grad_mlp_all = row_gather(grad_mlp)

    parts = 2
    hidden = act.shape[1] // parts
    out_folds = [
        Fold(act, grad_mlp_all, (f * hidden, 0), (hidden, D)) for f in range(parts)
    ]
    sent = []
    for mask in [near] + col_far[::-1]:
        for fold in out_folds:
            sent = [fold.step(1, "col", mask, *sent)]
    grad_pre = (
        col_product_back(after(grad_mlp_all, *sent), fc_out_near, fc_out_far)
        * gelu_slope(pre_act)
    ).astype(bf16)
    grad_fc_in_bias = jnp.sum(grad_pre, 0, dtype=f32)
    homes = [fold.home(1) for fold in out_folds]
    total_0 = homes[0] + out_folds[0].arrived[-1].astype(f32)
    low_0 = total_0.astype(bf16)
    in_0 = inward(low_0, bf16)
    grad_pre = after(grad_pre, low_0, homes[1])
    normed2_grads = jnp.concatenate([dot_nt(grad_pre, fc_in_near), dot_nt(grad_pre, fc_in_far)], 1)
    leaving = normed2_grads[own * count_row // 2 :].astype(bf16)
    arrived = send(leaving, "row", row_masks[-1])
    in_folds = [
        Fold(normed2_all, grad_pre, (0, f * hidden), (D, hidden)) for f in range(parts)
    ]
    sent = in_folds[0].step(0, "col", near, leaving)
    total_1 = homes[1] + after(out_folds[1].arrived[-1], sent).astype(f32)
    low_1 = total_1.astype(bf16)
    in_1 = inward(low_1, bf16)
    held_0, mid_0 = across_middle(total_0, after(in_0, sent), bf16)
    sent = [in_folds[1].step(0, "col", near, low_1, held_0)]
    for mask in col_far[::-1]:
        for fold in in_folds:
            sent = [fold.step(0, "col", mask, *sent)]
    homes_in = [fold.home(1) for fold in in_folds]
    grad_normed2 = normed2_grads[: own * count_row // 2] + after(
        arrived, *sent, *homes_in
    ).astype(f32)
    for mask in row_masks[:-1][::-1]:
        half = grad_normed2.shape[0] // 2
        grad_normed2 = grad_normed2[:half] + send(
            grad_normed2[half:].astype(bf16), "row", mask
        ).astype(f32)

    gain2_part = jnp.sum(grad_normed2 * normal2, 0)
    shift2_part = jnp.sum(grad_normed2, 0)
    grad_middle = grad_out + norm_backward(grad_normed2, normal2, inverse2, gain2)
    grad_attn = grad_middle.astype(bf16)
    grad_attn_bias = jnp.sum(grad_attn, 0, dtype=f32)
    total_2 = homes_in[0] + in_folds[0].arrived[-1].astype(f32)
    low_2 = total_2.astype(bf16)
    in_2 = inward(low_2, bf16)
    out_0 = outward(held_0, after(mid_0, grad_attn), bf16)
    held_1, mid_1 = across_middle(total_1, after(in_1, grad_attn), bf16)
    total_3 = homes_in[1] + after(in_folds[1].arrived[-1], grad_attn).astype(f32)
    low_3 = total_3.astype(bf16)
    in_3 = inward(low_3, bf16)

    attn_fold = Fold(attended, after(grad_attn, low_2, out_0[0], held_1))
    sent = attn_fold.step(1, "col", near)
    grad_attended = col_product_back(after(grad_attn, sent), attn_near, attn_far).astype(bf16)
    for mask in row_masks[::-1]:
        sent = attn_fold.step(0, "row", mask, sent)

    heads = queries.shape[1] // HEAD
    delta = jnp.sum(
        (attended.astype(f32) * grad_attended.astype(f32)).reshape(own, heads, HEAD), -1
    ).T
    grad_queries, grad_keys, grad_values = attend_backward(
        queries,
        after(grad_attended, low_3, sent),
        keys,
        values,
        limits,
        slots,
        log_totals,
        delta,
        chunk,
    )
    grad_keyval = jnp.concatenate([grad_keys, grad_values], 1)
    out_1 = outward(held_1, after(mid_1, grad_queries), bf16)
    held_2, mid_2 = across_middle(total_2, after(in_2, grad_queries), bf16)
    held_3, mid_3 = across_middle(total_3, after(in_3, grad_queries), bf16)

    query_fold = Fold(normed1, grad_queries)
    for mask in col_far[::-1]:
        sent_attn = attn_fold.step(1, "col", mask, grad_queries)
    sent = query_fold.step(0, "col", near, sent_attn)
    query_grads = jnp.concatenate([
        sum(
            dot_nt(
                after(grad_queries, sent, sent_attn)[:, i * wide : (i + 1) * wide],
                weights[i * split : (i + 1) * split],
            )
            for i in range(count_row)
        )
        for weights in (query_near, query_far)
    ], 1)
    for mask in row_masks[::-1]:
        sent = query_fold.step(1, "row", mask, sent, out_1[0], held_2)
    grad_keyval_low = halve_sum(after(grad_keyval, sent), all_out).astype(bf16)
    output_block = from_tokens(after(layer_output, sent), chunk, width, order)
    total_4 = attn_fold.home()
    low_4 = total_4.astype(bf16)
    in_4 = inward(low_4, bf16)
    out_2 = outward(held_2, after(mid_2, low_4), bf16)
    grad_value_bias = jnp.sum(grad_keyval_low[:, HEAD:], 0, dtype=f32)
    grad_query_bias = jnp.sum(grad_queries, 0, dtype=f32)
    for mask in col_far[::-1]:
        sent = query_fold.step(0, "col", mask, sent, held_3, low_4)

    grad_keyval_w = everywhere(
        halve_sum(dot_tn(normed1, grad_keyval_low), [step for step in all_out if step[0] == "col"]),
        ["row", "dp"],
    )
    grad_normed1 = query_grads + jnp.concatenate(
        [dot_nt(grad_keyval_low, keyval_near), dot_nt(grad_keyval_low, keyval_far)], 1
    )
    gain1_part = jnp.sum(grad_normed1 * normal1, 0)
    shift1_part = jnp.sum(grad_normed1, 0)
    input_grad = grad_middle + norm_backward(grad_normed1, normal1, inverse1, gain1)
    input_block = from_tokens(input_grad, chunk, width, order)

    held_4, mid_4 = across_middle(total_4, after(in_4, sent), bf16)
    out_3 = outward(held_3, after(mid_3, sent), bf16)
    total_5 = query_fold.home()
    in_5 = inward(after(total_5, out_3[0]).astype(bf16), bf16)
    out_4 = outward(held_4, mid_4, bf16)
    held_5, mid_5 = across_middle(total_5, in_5, bf16)
    out_5 = outward(held_5, mid_5, bf16)
    grad_query_w, grad_attn_out = settled(out_5), settled(out_4)
    out_0 = (out_0[0], after(out_0[1], grad_queries))
    grad_fc_out = jnp.concatenate([settled(out_0), settled(out_1)], 0)
    grad_fc_in = jnp.concatenate([settled(out_2), settled(out_3)], 1)

    unit = min(width, wide)
    per = width // unit
    feature_rows = jnp.stack(
        [gain1_part, shift1_part, gain2_part, shift2_part, grad_fc_out_bias, grad_attn_bias]
    )
    tail = jnp.concatenate([grad_value_bias, loss_part[None], jnp.zeros((unit - HEAD - 1,), f32)])
    shared = jnp.concatenate([tail, grad_query_bias, grad_fc_in_bias]).reshape(-1, unit)
    features = feature_rows.reshape(6, count_col, per, unit).transpose(1, 0, 2, 3)
    features = features.reshape(-1, unit)
    for mask in masks_of("col")[::-1]:
        half = features.shape[0] // 2
        came = send(jnp.concatenate([features[half:], shared], 0), "col", mask)
        features = features[:half] + came[:half]
        shared = shared + came[half:]
    ahead, each = 6 * per + 1, wide // unit
    pack = jnp.concatenate([features, shared], 0)
    query_sum = halve_sum(
        pack[ahead : ahead + count_row * each], [("row", mask) for mask in row_masks[::-1]]
    )
    hidden_rows = pack[ahead + count_row * each :]
    pack = jnp.concatenate([everywhere(pack[:ahead], ["row"]), query_sum, hidden_rows], 0)
    pack = everywhere(pack, ["dp"])
    vector_sums = [pack[k * per : (k + 1) * per].reshape(-1) for k in range(6)]
    value_bias_sum = pack[6 * per, :HEAD]
    loss_sum = pack[6 * per, HEAD]
    query_bias_sum = pack[ahead : ahead + each].reshape(-1)
    fc_in_bias_sum = pack[ahead + each :].reshape(-1)
    return (
        output_block,
        loss_sum / (valid_count * D),
        input_block,
        vector_sums[0],
        vector_sums[1],
        grad_query_w,
        query_bias_sum,
        grad_keyval_w,
        value_bias_sum,
        grad_attn_out,
        vector_sums[5],
        vector_sums[2],
        vector_sums[3],
        grad_fc_in,
        fc_in_bias_sum,
        grad_fc_out,
        vector_sums[4],
    )


def solution(mesh):
    placed = (
        P(("dp", "row"), "col"),
        P("col"),
        P("col"),
        P("col", "row"),
        P("row"),
        P("col", None),
        P(),
        P("row", "col"),
        P("col"),
        P("col"),
        P("col"),
        P("col", "row"),
        P("row"),
        P("row", "col"),
        P("col"),
        P("dp", None),
        P("dp", None),
        P(("dp", "row"), "col"),
        P(("dp", "row"), "col"),
    )
    return jax.shard_map(
        per_device,
        mesh=mesh,
        in_specs=placed,
        out_specs=(
            P(("dp", "row"), "col"),
            P(),
            P(("dp", "row"), "col"),
            P("col"),
            P("col"),
            P("col", "row"),
            P("row"),
            P("col", None),
            P(),
            P("row", "col"),
            P("col"),
            P("col"),
            P("col"),
            P("col", "row"),
            P("row"),
            P("row", "col"),
            P("col"),
        ),
        check_vma=False,
    )
```

```python
import functools
import jax, jax.numpy as jnp
from jax import lax
from jax.experimental import pallas as pl
from jax.experimental.pallas import tpu as pltpu
from jax.sharding import PartitionSpec as P

D = 2048
HEAD = 128
SCALE = HEAD**-0.5
SC = SCALE * 1.4426950408889634
NT = (((1,), (1,)), ((), ()))
NN = (((1,), (0,)), ((), ()))
TN = (((0,), (0,)), ((), ()))
f32 = jnp.float32
bf16 = jnp.bfloat16


def stack_heads(ref, heads):
    return jnp.concatenate([ref[:, h * HEAD : (h + 1) * HEAD] for h in range(heads)], axis=0)


def key_rows(ref, slot_ref, block, per_block, chunk):
    parts = [
        ref[pl.ds(pl.multiple_of(slot_ref[block * per_block + s] * chunk, chunk), chunk), :]
        for s in range(per_block)
    ]
    return parts[0] if per_block == 1 else jnp.concatenate(parts, axis=0)


def fwd_kernel(
    full_ref, count_ref, slot_ref, q_ref, k_ref, v_ref, lim_ref, o_ref, lse_ref, acc, top, tot,
    *, heads, tq, chunk, per_block
):
    t = pl.program_id(0)
    bk = chunk * per_block
    q = stack_heads(q_ref, heads)
    acc[...] = jnp.zeros_like(acc)
    top[...] = jnp.full_like(top, -1e30)
    tot[...] = jnp.zeros_like(tot)

    def step(block, masked):
        kk = key_rows(k_ref, slot_ref, block, per_block, chunk)
        vv = key_rows(v_ref, slot_ref, block, per_block, chunk)
        s = lax.dot_general(kk, q, NT, preferred_element_type=f32)
        if masked:
            ids = lax.broadcasted_iota(jnp.int32, (bk, heads * tq), 0) + block * bk
            lim = jnp.concatenate([lim_ref[:1, :]] * heads, axis=1)
            s = jnp.where(ids < lim, s, -1e30)
        before = top[...]
        now = jnp.maximum(before, jnp.max(s, axis=0, keepdims=True))
        p = jnp.exp2(s * SC - now * SC)
        top[...] = now
        a = jnp.exp2((before - now) * SC)
        tot[...] = tot[...] * a + jnp.sum(p, axis=0, keepdims=True)
        acc[...] = acc[...] * a + lax.dot_general(
            vv, p.astype(bf16), TN, preferred_element_type=f32
        )

    lax.fori_loop(0, full_ref[t], lambda b, c: (step(b, False), c)[1], 0)
    lax.fori_loop(full_ref[t], count_ref[t], lambda b, c: (step(b, True), c)[1], 0)
    o = acc[...] * (1.0 / tot[...])
    lse = top[...] * SC + jnp.log2(tot[...])
    for h in range(heads):
        o_ref[:, h * HEAD : (h + 1) * HEAD] = jnp.transpose(o[:, h * tq : (h + 1) * tq]).astype(bf16)
        lse_ref[h : h + 1, :] = lse[:, h * tq : (h + 1) * tq]


def bwd_kernel(
    full_ref, count_ref, slot_ref, q_ref, do_ref, k_ref, v_ref, lim_ref, lse_ref, dl_ref,
    dq_ref, dk_ref, dv_ref, dqa, *, heads, tq, chunk, per_block
):
    t = pl.program_id(0)
    bk = chunk * per_block

    @pl.when((t == 0) & (pl.program_id(1) == 0))
    def _():
        dk_ref[...] = jnp.zeros_like(dk_ref)
        dv_ref[...] = jnp.zeros_like(dv_ref)

    q = stack_heads(q_ref, heads)
    do = stack_heads(do_ref, heads)
    lse = jnp.concatenate([lse_ref[h : h + 1, :] for h in range(heads)], axis=1)
    dl = jnp.concatenate([dl_ref[h : h + 1, :] for h in range(heads)], axis=1)
    dqa[...] = jnp.zeros_like(dqa)

    def step(block, masked):
        kk = key_rows(k_ref, slot_ref, block, per_block, chunk)
        vv = key_rows(v_ref, slot_ref, block, per_block, chunk)
        s = lax.dot_general(kk, q, NT, preferred_element_type=f32)
        p = jnp.exp2(s * SC - lse)
        if masked:
            ids = lax.broadcasted_iota(jnp.int32, (bk, heads * tq), 0) + block * bk
            lim = jnp.concatenate([lim_ref[:1, :]] * heads, axis=1)
            p = jnp.where(ids < lim, p, 0.0)
        dp = lax.dot_general(vv, do, NT, preferred_element_type=f32)
        ds = (p * (dp - dl)).astype(bf16)
        dv = lax.dot_general(p.astype(bf16), do, NN, preferred_element_type=f32)
        dk = lax.dot_general(ds, q, NN, preferred_element_type=f32)
        dqa[...] += lax.dot_general(ds, kk, TN, preferred_element_type=f32)
        for s in range(per_block):
            off = pl.multiple_of(slot_ref[block * per_block + s] * chunk, chunk)
            dk_ref[pl.ds(off, chunk), :] += dk[s * chunk : (s + 1) * chunk]
            dv_ref[pl.ds(off, chunk), :] += dv[s * chunk : (s + 1) * chunk]

    lax.fori_loop(0, full_ref[t], lambda b, c: (step(b, False), c)[1], 0)
    lax.fori_loop(full_ref[t], count_ref[t], lambda b, c: (step(b, True), c)[1], 0)
    dq = (dqa[...] * HEAD**-0.5).astype(bf16)
    for h in range(heads):
        dq_ref[:, h * HEAD : (h + 1) * HEAD] = dq[h * tq : (h + 1) * tq]

    @pl.when((t == pl.num_programs(0) - 1) & (pl.program_id(1) == pl.num_programs(1) - 1))
    def _():
        dk_ref[...] = dk_ref[...] * HEAD**-0.5


def block_counts(limits, tq, bk):
    tiles = limits.reshape(-1, tq)
    return jnp.min(tiles, 1) // bk, (jnp.max(tiles, 1) + bk - 1) // bk


def attend_forward(q, k, v, limits, slots, chunk, tq=128, heads=16, bk=256):
    n, hq = q.shape
    total = hq // HEAD
    per_block = max(1, bk // chunk)
    full, count = block_counts(limits, tq, chunk * per_block)
    rows = k.shape[0]
    grid = pltpu.PrefetchScalarGridSpec(
        num_scalar_prefetch=3,
        grid=(n // tq, total // heads),
        in_specs=[
            pl.BlockSpec((tq, heads * HEAD), lambda t, g, *_: (t, g)),
            pl.BlockSpec((rows, HEAD), lambda t, g, *_: (0, 0)),
            pl.BlockSpec((rows, HEAD), lambda t, g, *_: (0, 0)),
            pl.BlockSpec((8, tq), lambda t, g, *_: (0, t)),
        ],
        out_specs=[
            pl.BlockSpec((tq, heads * HEAD), lambda t, g, *_: (t, g)),
            pl.BlockSpec((heads, tq), lambda t, g, *_: (g, t)),
        ],
        scratch_shapes=[
            pltpu.VMEM((HEAD, heads * tq), f32),
            pltpu.VMEM((1, heads * tq), f32),
            pltpu.VMEM((1, heads * tq), f32),
        ],
    )
    return pl.pallas_call(
        functools.partial(fwd_kernel, heads=heads, tq=tq, chunk=chunk, per_block=per_block),
        grid_spec=grid,
        out_shape=(jax.ShapeDtypeStruct((n, hq), bf16), jax.ShapeDtypeStruct((total, n), f32)),
        name="attend_forward",
        compiler_params=pltpu.CompilerParams(vmem_limit_bytes=48 << 20),
    )(full, count, slots, q, k, v, jnp.broadcast_to(limits[None, :], (8, n)))


def attend_backward(q, do, k, v, limits, slots, lse, delta, chunk, tq=128, heads=16, bk=256):
    n, hq = q.shape
    total = hq // HEAD
    per_block = max(1, bk // chunk)
    full, count = block_counts(limits, tq, chunk * per_block)
    rows = k.shape[0]
    token_block = pl.BlockSpec((tq, heads * HEAD), lambda t, g, *_: (t, g))
    key_block = pl.BlockSpec((rows, HEAD), lambda t, g, *_: (0, 0))
    head_block = pl.BlockSpec((heads, tq), lambda t, g, *_: (g, t))
    grid = pltpu.PrefetchScalarGridSpec(
        num_scalar_prefetch=3,
        grid=(n // tq, total // heads),
        in_specs=[
            token_block, token_block, key_block, key_block,
            pl.BlockSpec((8, tq), lambda t, g, *_: (0, t)),
            head_block, head_block,
        ],
        out_specs=[token_block, key_block, key_block],
        scratch_shapes=[pltpu.VMEM((heads * tq, HEAD), f32)],
    )
    return pl.pallas_call(
        functools.partial(bwd_kernel, heads=heads, tq=tq, chunk=chunk, per_block=per_block),
        grid_spec=grid,
        out_shape=(
            jax.ShapeDtypeStruct((n, hq), bf16),
            jax.ShapeDtypeStruct((rows, HEAD), f32),
            jax.ShapeDtypeStruct((rows, HEAD), f32),
        ),
        name="attend_backward",
        compiler_params=pltpu.CompilerParams(vmem_limit_bytes=48 << 20),
    )(full, count, slots, q, do, k, v, jnp.broadcast_to(limits[None, :], (8, n)), lse, delta)


epsilon = 1e-05
gelu_coeff = 0.7978845608028654


def send(x, axis, mask):
    size = lax.axis_size(axis)
    return lax.ppermute(x, axis, [(i, i ^ mask) for i in range(size)])


def send_pair(x, i, j):
    count_row, count_col = lax.axis_size("row"), lax.axis_size("col")
    pairs = [
        (a * count_col + b, (a ^ i) * count_col + (b ^ j))
        for a in range(count_row)
        for b in range(count_col)
    ]
    return lax.ppermute(x, ("row", "col"), pairs)


def masks_of(axis):
    size = lax.axis_size(axis)
    return [1 << k for k in reversed(range(size.bit_length() - 1))]


def other_key(key, axis, mask):
    return (key[0] ^ mask, key[1]) if axis == "row" else (key[0], key[1] ^ mask)


def grow(parts, axis, masks):
    for mask in masks:
        parts = parts + [send(part, axis, mask) for part in parts]
    return parts


def product_kernel(*refs):
    left, right, *others, out = refs
    made = lax.dot_general(left[...], right[...], TN, preferred_element_type=f32)
    for other in others:
        made = made + other[...].astype(f32)
    out[...] = made.astype(out.dtype)


def token_product(left, right, rows, cols, base, others, kind):
    tokens = left.shape[0]
    tall, broad = min(512, rows[1] - rows[0]), min(1024, cols[1] - cols[0])
    left_at, right_at = (base[0] + rows[0]) // tall, (base[1] + cols[0]) // broad
    row_at, col_at = rows[0] // tall, cols[0] // broad
    return pl.pallas_call(
        product_kernel,
        grid=((rows[1] - rows[0]) // tall, (cols[1] - cols[0]) // broad),
        in_specs=[
            pl.BlockSpec((tokens, tall), lambda i, j: (0, left_at + i)),
            pl.BlockSpec((tokens, broad), lambda i, j: (0, right_at + j)),
        ]
        + [pl.BlockSpec((tall, broad), lambda i, j: (row_at + i, col_at + j)) for _ in others],
        out_specs=pl.BlockSpec((tall, broad), lambda i, j: (i, j)),
        out_shape=jax.ShapeDtypeStruct((rows[1] - rows[0], cols[1] - cols[0]), kind),
        name="token_product",
        compiler_params=pltpu.CompilerParams(vmem_limit_bytes=48 << 20),
    )(left, right, *others)


class Fold:
    def __init__(self, left, right, base=(0, 0), size=None):
        self.left, self.right, self.base, self.arrived = left, right, base, []
        self.limits = list(size or (left.shape[1], right.shape[1]))

    def part(self, rows, cols, kind):
        return token_product(self.left, self.right, rows, cols, self.base, self.arrived, kind)

    def step(self, dim, axis, mask, *needed):
        if needed:
            self.left = after(self.left, *needed)
        half = self.limits[dim] // 2
        spans = [(0, self.limits[0]), (0, self.limits[1])]
        spans[dim] = (half, self.limits[dim])
        leaving = self.part(*spans, bf16)
        self.arrived = self.arrived + [send(leaving, axis, mask)]
        self.limits[dim] = half
        return leaving

    def home(self, skip=0):
        kept = self.arrived
        self.arrived = kept[: len(kept) - skip]
        made = self.part((0, self.limits[0]), (0, self.limits[1]), f32)
        self.arrived = kept
        return made


def halve_sum(x, steps):
    for axis, mask in steps:
        half = x.shape[0] // 2
        x = x[:half] + send(x[half:], axis, mask)
    return x


def after(x, *needed):
    return lax.optimization_barrier((x,) + needed)[0]


def everywhere(x, axes):
    for axis in axes:
        for mask in masks_of(axis):
            x = x + send(x, axis, mask)
    return x


def gelu_tanh(values):
    return (
        0.5 * values * (1.0 + jnp.tanh(gelu_coeff * (values + 0.044715 * values * values * values)))
    )


def gelu_slope(values):
    square = values * values
    curve = jnp.tanh(gelu_coeff * values * (1.0 + 0.044715 * square))
    return 0.5 * (1.0 + curve) + 0.5 * values * (1.0 - curve * curve) * gelu_coeff * (
        1.0 + 3.0 * 0.044715 * square
    )


def norm_forward(values, gain, shift):
    means = jnp.mean(values, 1, keepdims=True)
    squares = jnp.mean(values * values, 1, keepdims=True)
    inverse = lax.rsqrt(squares - means * means + epsilon)
    normal = (values - means) * inverse
    return (normal, inverse, (normal * gain + shift).astype(bf16))


def norm_backward(grad, normal, inverse, gain):
    scaled = grad * gain
    return inverse * (
        scaled
        - jnp.mean(scaled, 1, keepdims=True)
        - normal * jnp.mean(scaled * normal, 1, keepdims=True)
    )


def dot_nn(a, b):
    return lax.dot_general(a, b, NN, preferred_element_type=f32)


def dot_nt(a, b):
    return lax.dot_general(a, b, NT, preferred_element_type=f32)


def dot_tn(a, b):
    return lax.dot_general(a, b, TN, preferred_element_type=f32)


def flips():
    if lax.axis_size("row") == 2:
        return [lax.axis_index("row") ^ i for i in range(2)]
    return [0, 1]


def pick(halves, bit):
    rows = halves.shape[0] // 2
    return [
        lax.dynamic_slice_in_dim(halves, jnp.where(bit == stay, 0, rows), rows, 0)
        for stay in (0, 1)
    ]


def place_bits(mask):
    count_col = lax.axis_size("col")
    col = lax.axis_index("col")
    return [jnp.where((col ^ ((count_col - 1) * flip)) & mask, 1, 0) for flip in flips()]


def to_tokens_direct(block, chunk):
    count_row, count_col = lax.axis_size("row"), lax.axis_size("col")
    out = {}
    for i in range(2):
        for j in range(count_col):
            flip = lax.axis_index("row") if count_row == 2 else i
            place = lax.axis_index("col") ^ j ^ ((count_col - 1) * flip)
            part = lax.dynamic_slice_in_dim(block, (i * count_col + place) * chunk, chunk, 0)
            if count_row == 2:
                out[(i, j)] = send_pair(part, i, j) if i or j else part
            else:
                out[(i, j)] = send(part, "col", j) if j else part
    return out


def to_tokens(block, chunk, waits):
    half = block.shape[0] // 2
    lower, upper = block[:half], block[half:]
    if lax.axis_size("row") == 2:
        upper = send(after(upper, waits[0]), "row", 1)
    groups = {(0, 0): lower, (1, 0): upper}
    for mask, wait in zip(masks_of("col"), waits[1:]):
        groups[(1, 0)] = after(groups[(1, 0)], wait)
        bits = place_bits(mask)
        leaving = []
        for key in list(groups):
            groups[key], gone = pick(groups[key], bits[key[0]])
            leaving.append(gone)
        arrived = send(jnp.concatenate(leaving, 0), "col", mask)
        rows = leaving[0].shape[0]
        for k, key in enumerate(list(groups)):
            groups[(key[0], key[1] ^ mask)] = arrived[k * rows : (k + 1) * rows]
    return groups


def assemble(groups, order):
    return jnp.concatenate(
        [jnp.concatenate([groups[(i, j)] for j in order], 1) for i in range(2)], 0
    )


def from_tokens(tokens, chunk, width, order):
    low = tokens.astype(bf16)
    groups = {
        (i, j): low[i * chunk : (i + 1) * chunk, k * width : (k + 1) * width]
        for i in range(2)
        for k, j in enumerate(order)
    }
    for mask in masks_of("col")[::-1]:
        bits = place_bits(mask)
        leaving = [key for key in groups if key[1] & mask]
        rows = groups[leaving[0]].shape[0]
        arrived = send(jnp.concatenate([groups[key] for key in leaving], 0), "col", mask)
        for k, key in enumerate(leaving):
            del groups[key]
            kept = groups[(key[0], key[1] ^ mask)]
            came = arrived[k * rows : (k + 1) * rows]
            swap = bits[key[0]] == 1
            groups[(key[0], key[1] ^ mask)] = jnp.concatenate(
                [jnp.where(swap, came, kept), jnp.where(swap, kept, came)], 0
            )
    upper = groups[(1, 0)]
    if lax.axis_size("row") == 2:
        upper = send(upper, "row", 1)
    return jnp.concatenate([groups[(0, 0)], upper], 0).astype(f32)


def token_starts(chunk):
    count_row, count_col = lax.axis_size("row"), lax.axis_size("col")
    r, c = lax.axis_index("row"), lax.axis_index("col")
    if count_row == 2:
        own = r * count_col + c
        low, high = own * chunk, (4 * count_col - 1 - own) * chunk
        return [jnp.where(r == 0, low, high), jnp.where(r == 0, high, low)]
    return [(r * 2 * count_col + c) * chunk, (r * 2 * count_col + 2 * count_col - 1 - c) * chunk]


def key_slots():
    count_row, count_col = lax.axis_size("row"), lax.axis_size("col")
    r, c = lax.axis_index("row"), lax.axis_index("col")
    group = jnp.arange(2 * count_row * count_col, dtype=jnp.int32)
    half = group // (2 * count_col)
    if count_row == 2:
        owner = jnp.where(half == 0, group, 4 * count_col - 1 - group)
        owner_row, owner_col = owner // count_col, owner % count_col
        which = owner_row ^ half
    else:
        local = group % (2 * count_col)
        owner_row = half
        which = (local >= count_col).astype(jnp.int32)
        owner_col = jnp.where(which == 0, local, 2 * count_col - 1 - local)
    place = jnp.zeros_like(group)
    for k, (axis, mask) in enumerate(gather_steps()):
        relative = owner_row ^ r if axis == "row" else owner_col ^ c
        place = place + jnp.where(relative & mask, 1 << k, 0)
    return place * 2 + which


def gather_steps():
    col = [("col", mask) for mask in masks_of("col")]
    return col[:-1] + [("row", mask) for mask in masks_of("row")] + col[-1:]


def inward(total, wire):
    if lax.axis_size("dp") != 4:
        return total
    return lax.ppermute(total.astype(wire), "dp", [(0, 1), (3, 2)])


def across_middle(total, arrived, wire):
    if lax.axis_size("dp") != 4:
        return (total, total)
    held = (total + arrived.astype(f32)).astype(wire)
    return (held, lax.ppermute(held, "dp", [(1, 2), (2, 1)]))


def outward(held, arrived, wire):
    if lax.axis_size("dp") != 4:
        final = everywhere(held.astype(f32), ["dp"])
        return (final, final)
    final = (held.astype(f32) + arrived.astype(f32)).astype(wire)
    return (final, lax.ppermute(final, "dp", [(1, 0), (2, 3)]))


def settled(pair):
    final, end = pair
    if lax.axis_size("dp") != 4:
        return final
    z = lax.axis_index("dp")
    return jnp.where((z == 1) | (z == 2), final, end).astype(f32)


def per_device(
    layer_input,
    norm1_gain,
    norm1_shift,
    w_query,
    b_query,
    w_keyval,
    b_value,
    w_attn_out,
    b_attn_out,
    norm2_gain,
    norm2_shift,
    w_fc_in,
    b_fc_in,
    w_fc_out,
    b_fc_out,
    valid_mask,
    block_ids,
    teacher,
    out_cotangent,
):
    count_row = lax.axis_size("row")
    count_col = lax.axis_size("col")
    count_dp = lax.axis_size("dp")
    rows_a, width = layer_input.shape
    wide = w_query.shape[1]
    chunk = rows_a // (2 * count_col)
    col_far, near = masks_of("col")[:-1], masks_of("col")[-1]
    row_masks = masks_of("row")
    all_out = gather_steps()[::-1]
    order = [0]
    for mask in masks_of("col"):
        order = order + [j ^ mask for j in order]
    split = D // 2
    valid_flat = valid_mask.reshape(-1)
    block_flat = block_ids.reshape(-1)

    x_groups = to_tokens_direct(layer_input, chunk)
    keyval_near = jnp.concatenate(grow([w_keyval], "col", col_far), 0)
    keyval_far = send(keyval_near, "col", near)
    vectors = jnp.stack(
        [norm1_gain, norm1_shift, b_attn_out, norm2_gain, norm2_shift, b_fc_out]
    )
    vectors = jnp.concatenate(grow([vectors], "col", col_far), 1)
    vectors = jnp.concatenate([vectors, send(vectors, "col", near)], 1)
    gain1, shift1, bias_o, gain2, shift2, bias_out = [vectors[k : k + 1] for k in range(6)]
    bias_q = jnp.concatenate(grow([b_query[None, :]], "row", row_masks), 1)

    starts = token_starts(chunk)
    block_own = jnp.concatenate(
        [lax.dynamic_slice_in_dim(block_flat, start, chunk, 0) for start in starts]
    )
    valid_own = jnp.concatenate(
        [lax.dynamic_slice_in_dim(valid_flat, start, chunk, 0) for start in starts]
    ).astype(f32)[:, None]
    valid_length = jnp.sum(valid_flat)
    reach = jnp.sum((block_flat[None, :] <= block_own[:, None]).astype(jnp.int32), 1)
    limits = jnp.minimum(reach, valid_length)
    slots = key_slots()

    residual = assemble(x_groups, order).astype(f32)
    normal1, inverse1, normed1 = norm_forward(residual, gain1, shift1)
    query_cols = grow([after(w_query, *x_groups.values())], "col", col_far)
    query_cols = query_cols[:1] + [after(part, normed1) for part in query_cols[1:]]
    keyval = dot_nn(normed1[:, :split], keyval_near) + dot_nn(normed1[:, split:], keyval_far)
    keyval = jnp.concatenate(
        [keyval[:, :HEAD].astype(bf16), (keyval[:, HEAD:] + b_value).astype(bf16)], 1
    )
    keyval_far_rows = grow([keyval], "col", col_far)
    query_rows = [grow([part], "row", row_masks) for part in query_cols]
    query_parts = [
        jnp.concatenate([after(part, keyval) for part in parts], 0) for parts in zip(*query_rows)
    ]
    query_near = jnp.concatenate(query_parts, 0)
    query_far = send(query_near, "col", near)
    keyval_all = jnp.concatenate(keyval_far_rows, 0)
    keyval_all = jnp.concatenate(grow([keyval_all], "row", row_masks), 0)
    keyval_all = jnp.concatenate([keyval_all, send(keyval_all, "col", near)], 0)
    attn_cols = grow([after(w_attn_out, keyval_far_rows[-1])], "col", col_far)
    fc_in_rows = grow([after(w_fc_in, attn_cols[-1])], "col", col_far)
    keys, values = keyval_all[:, :HEAD], keyval_all[:, HEAD:]
    queries = jnp.concatenate(
        [
            dot_nn(normed1[:, :split], query_near[i * split : (i + 1) * split])
            + dot_nn(normed1[:, split:], query_far[i * split : (i + 1) * split])
            for i in range(count_row)
        ],
        1,
    )
    queries = (queries + bias_q).astype(bf16)
    attn_rows = grow([after(jnp.concatenate(attn_cols, 1), queries)], "row", row_masks)
    fc_out_cols = grow([after(w_fc_out, queries)], "col", col_far)
    attended, log_totals = attend_forward(queries, keys, values, limits, slots, chunk)
    attn_near = jnp.concatenate(attn_rows[:-1] + [after(attn_rows[-1], attended)], 0)
    attn_far = send(attn_near, "col", near)
    middle_first = dot_nn(attended, attn_near)
    middle = jnp.concatenate([middle_first, dot_nn(attended, attn_far)], 1)
    middle = residual + (middle + bias_o)
    normal2, inverse2, normed2 = norm_forward(middle, gain2, shift2)
    own = normed2.shape[0]
    fc_in_near = jnp.concatenate(fc_in_rows[:-1] + [after(fc_in_rows[-1], middle_first, attn_far)], 0)
    fc_in_far = send(fc_in_near, "col", near)

    def col_product(x, first, second):
        return dot_nn(x[:, :split], first) + dot_nn(x[:, split:], second)

    def col_product_back(x, first, second):
        return dot_nt(x[:, :split], first) + dot_nt(x[:, split:], second)

    def row_gather(x):
        return jnp.concatenate(grow([x], "row", row_masks), 0)

    def row_sum(x):
        for mask in row_masks[::-1]:
            half = x.shape[0] // 2
            x = x[:half] + send(x[half:].astype(bf16), "row", mask).astype(f32)
        return x

    normed2_all = row_gather(normed2)
    pre_act = col_product(normed2_all, fc_in_near, fc_in_far) + b_fc_in
    act = gelu_tanh(pre_act).astype(bf16)
    fc_out_near = jnp.concatenate(fc_out_cols[:-1] + [after(fc_out_cols[-1], act)], 1)
    fc_out_far = send(fc_out_near, "col", near)
    fc_out_first = dot_nn(act, fc_out_near)
    fc_out_parts = jnp.concatenate([fc_out_first, dot_nn(act, fc_out_far)], 1)
    fc_out_sum = row_sum(fc_out_parts)
    layer_output = middle + (fc_out_sum + bias_out)
    valid_count = jnp.full((8, 128), valid_length.astype(f32))
    valid_count = everywhere(after(valid_count, attended), ["dp"])[0, 0]
    late_groups = [
        to_tokens(block, chunk, [act, fc_out_first, fc_out_sum])
        for block in (teacher, out_cotangent)
    ]
    target = assemble(late_groups[0], order)
    cotangent = assemble(late_groups[1], order)
    errors = layer_output - target.astype(f32)
    loss_part = jnp.sum(valid_own * errors * errors)
    ratio = rows_a * count_row * count_dp / valid_count
    grad_out = cotangent.astype(f32) + ratio * valid_own * errors
    grad_mlp = grad_out.astype(bf16)
    grad_fc_out_bias = jnp.sum(grad_mlp, 0, dtype=f32)
    grad_mlp_all = row_gather(grad_mlp)

    parts = 2
    hidden = act.shape[1] // parts
    out_folds = [
        Fold(act, grad_mlp_all, (f * hidden, 0), (hidden, D)) for f in range(parts)
    ]
    sent = []
    for mask in [near] + col_far[::-1]:
        for fold in out_folds:
            sent = [fold.step(1, "col", mask, *sent)]
    grad_pre = (
        col_product_back(after(grad_mlp_all, *sent), fc_out_near, fc_out_far)
        * gelu_slope(pre_act)
    ).astype(bf16)
    grad_fc_in_bias = jnp.sum(grad_pre, 0, dtype=f32)
    homes = [fold.home(1) for fold in out_folds]
    total_0 = homes[0] + out_folds[0].arrived[-1].astype(f32)
    low_0 = total_0.astype(bf16)
    in_0 = inward(low_0, bf16)
    grad_pre = after(grad_pre, low_0, homes[1])
    normed2_grads = jnp.concatenate([dot_nt(grad_pre, fc_in_near), dot_nt(grad_pre, fc_in_far)], 1)
    leaving = normed2_grads[own * count_row // 2 :].astype(bf16)
    arrived = send(leaving, "row", row_masks[-1])
    in_folds = [
        Fold(normed2_all, grad_pre, (0, f * hidden), (D, hidden)) for f in range(parts)
    ]
    sent = in_folds[0].step(0, "col", near, leaving)
    total_1 = homes[1] + after(out_folds[1].arrived[-1], sent).astype(f32)
    low_1 = total_1.astype(bf16)
    in_1 = inward(low_1, bf16)
    held_0, mid_0 = across_middle(total_0, after(in_0, sent), bf16)
    sent = [in_folds[1].step(0, "col", near, low_1, held_0)]
    for mask in col_far[::-1]:
        for fold in in_folds:
            sent = [fold.step(0, "col", mask, *sent)]
    homes_in = [fold.home(1) for fold in in_folds]
    grad_normed2 = normed2_grads[: own * count_row // 2] + after(
        arrived, *sent, *homes_in
    ).astype(f32)
    for mask in row_masks[:-1][::-1]:
        half = grad_normed2.shape[0] // 2
        grad_normed2 = grad_normed2[:half] + send(
            grad_normed2[half:].astype(bf16), "row", mask
        ).astype(f32)

    gain2_part = jnp.sum(grad_normed2 * normal2, 0)
    shift2_part = jnp.sum(grad_normed2, 0)
    grad_middle = grad_out + norm_backward(grad_normed2, normal2, inverse2, gain2)
    grad_attn = grad_middle.astype(bf16)
    grad_attn_bias = jnp.sum(grad_attn, 0, dtype=f32)
    total_2 = homes_in[0] + in_folds[0].arrived[-1].astype(f32)
    low_2 = total_2.astype(bf16)
    in_2 = inward(low_2, bf16)
    out_0 = outward(held_0, after(mid_0, grad_attn), bf16)
    held_1, mid_1 = across_middle(total_1, after(in_1, grad_attn), bf16)
    total_3 = homes_in[1] + after(in_folds[1].arrived[-1], grad_attn).astype(f32)
    low_3 = total_3.astype(bf16)
    in_3 = inward(low_3, bf16)

    attn_fold = Fold(attended, after(grad_attn, low_2, out_0[0], held_1))
    sent = attn_fold.step(1, "col", near)
    grad_attended = col_product_back(after(grad_attn, sent), attn_near, attn_far).astype(bf16)
    for mask in row_masks[::-1]:
        sent = attn_fold.step(0, "row", mask, sent)

    heads = queries.shape[1] // HEAD
    delta = jnp.sum(
        (attended.astype(f32) * grad_attended.astype(f32)).reshape(own, heads, HEAD), -1
    ).T
    grad_queries, grad_keys, grad_values = attend_backward(
        queries,
        after(grad_attended, low_3, sent),
        keys,
        values,
        limits,
        slots,
        log_totals,
        delta,
        chunk,
    )
    grad_keyval = jnp.concatenate([grad_keys, grad_values], 1)
    out_1 = outward(held_1, after(mid_1, grad_queries), bf16)
    held_2, mid_2 = across_middle(total_2, after(in_2, grad_queries), bf16)
    held_3, mid_3 = across_middle(total_3, after(in_3, grad_queries), bf16)

    query_fold = Fold(normed1, grad_queries)
    for mask in col_far[::-1]:
        sent_attn = attn_fold.step(1, "col", mask, grad_queries)
    sent = query_fold.step(0, "col", near, sent_attn)
    query_grads = jnp.concatenate([
        sum(
            dot_nt(
                after(grad_queries, sent, sent_attn)[:, i * wide : (i + 1) * wide],
                weights[i * split : (i + 1) * split],
            )
            for i in range(count_row)
        )
        for weights in (query_near, query_far)
    ], 1)
    for mask in row_masks[::-1]:
        sent = query_fold.step(1, "row", mask, sent, out_1[0], held_2)
    grad_keyval_low = halve_sum(after(grad_keyval, sent), all_out).astype(bf16)
    output_block = from_tokens(after(layer_output, sent), chunk, width, order)
    total_4 = attn_fold.home()
    low_4 = total_4.astype(bf16)
    in_4 = inward(low_4, bf16)
    out_2 = outward(held_2, after(mid_2, low_4), bf16)
    grad_value_bias = jnp.sum(grad_keyval_low[:, HEAD:], 0, dtype=f32)
    grad_query_bias = jnp.sum(grad_queries, 0, dtype=f32)
    for mask in col_far[::-1]:
        sent = query_fold.step(0, "col", mask, sent, held_3, low_4)

    grad_keyval_w = everywhere(
        halve_sum(dot_tn(normed1, grad_keyval_low), [step for step in all_out if step[0] == "col"]),
        ["row", "dp"],
    )
    grad_normed1 = query_grads + jnp.concatenate(
        [dot_nt(grad_keyval_low, keyval_near), dot_nt(grad_keyval_low, keyval_far)], 1
    )
    gain1_part = jnp.sum(grad_normed1 * normal1, 0)
    shift1_part = jnp.sum(grad_normed1, 0)
    input_grad = grad_middle + norm_backward(grad_normed1, normal1, inverse1, gain1)
    input_block = from_tokens(input_grad, chunk, width, order)

    held_4, mid_4 = across_middle(total_4, after(in_4, sent), bf16)
    out_3 = outward(held_3, after(mid_3, sent), bf16)
    total_5 = query_fold.home()
    in_5 = inward(after(total_5, out_3[0]).astype(bf16), bf16)
    out_4 = outward(held_4, mid_4, bf16)
    held_5, mid_5 = across_middle(total_5, in_5, bf16)
    out_5 = outward(held_5, mid_5, bf16)
    grad_query_w, grad_attn_out = settled(out_5), settled(out_4)
    out_0 = (out_0[0], after(out_0[1], grad_queries))
    grad_fc_out = jnp.concatenate([settled(out_0), settled(out_1)], 0)
    grad_fc_in = jnp.concatenate([settled(out_2), settled(out_3)], 1)

    unit = min(width, wide)
    per = width // unit
    feature_rows = jnp.stack(
        [gain1_part, shift1_part, gain2_part, shift2_part, grad_fc_out_bias, grad_attn_bias]
    )
    tail = jnp.concatenate([grad_value_bias, loss_part[None], jnp.zeros((unit - HEAD - 1,), f32)])
    shared = jnp.concatenate([tail, grad_query_bias, grad_fc_in_bias]).reshape(-1, unit)
    features = feature_rows.reshape(6, count_col, per, unit).transpose(1, 0, 2, 3)
    features = features.reshape(-1, unit)
    for mask in masks_of("col")[::-1]:
        half = features.shape[0] // 2
        came = send(jnp.concatenate([features[half:], shared], 0), "col", mask)
        features = features[:half] + came[:half]
        shared = shared + came[half:]
    ahead, each = 6 * per + 1, wide // unit
    pack = jnp.concatenate([features, shared], 0)
    query_sum = halve_sum(
        pack[ahead : ahead + count_row * each], [("row", mask) for mask in row_masks[::-1]]
    )
    hidden_rows = pack[ahead + count_row * each :]
    pack = jnp.concatenate([everywhere(pack[:ahead], ["row"]), query_sum, hidden_rows], 0)
    pack = everywhere(pack, ["dp"])
    vector_sums = [pack[k * per : (k + 1) * per].reshape(-1) for k in range(6)]
    value_bias_sum = pack[6 * per, :HEAD]
    loss_sum = pack[6 * per, HEAD]
    query_bias_sum = pack[ahead : ahead + each].reshape(-1)
    fc_in_bias_sum = pack[ahead + each :].reshape(-1)
    return (
        output_block,
        loss_sum / (valid_count * D),
        input_block,
        vector_sums[0],
        vector_sums[1],
        grad_query_w,
        query_bias_sum,
        grad_keyval_w,
        value_bias_sum,
        grad_attn_out,
        vector_sums[5],
        vector_sums[2],
        vector_sums[3],
        grad_fc_in,
        fc_in_bias_sum,
        grad_fc_out,
        vector_sums[4],
    )


def solution(mesh):
    placed = (
        P(("dp", "row"), "col"),
        P("col"),
        P("col"),
        P("col", "row"),
        P("row"),
        P("col", None),
        P(),
        P("row", "col"),
        P("col"),
        P("col"),
        P("col"),
        P("col", "row"),
        P("row"),
        P("row", "col"),
        P("col"),
        P("dp", None),
        P("dp", None),
        P(("dp", "row"), "col"),
        P(("dp", "row"), "col"),
    )
    return jax.shard_map(
        per_device,
        mesh=mesh,
        in_specs=placed,
        out_specs=(
            P(("dp", "row"), "col"),
            P(),
            P(("dp", "row"), "col"),
            P("col"),
            P("col"),
            P("col", "row"),
            P("row"),
            P("col", None),
            P(),
            P("row", "col"),
            P("col"),
            P("col"),
            P("col"),
            P("col", "row"),
            P("row"),
            P("row", "col"),
            P("col"),
        ),
        check_vma=False,
    )
```
